1024 devices in a mesh: row: 64 (over z, core), col: 16 (over x, y).
Axes of the slice: x: 4, y: 4, z: 32, core: 2. Of those that a mesh axis runs over, the one named last changes fastest.
Arguments:
- spans: bfloat16 [32768, 768], P(('row', 'col')), may hold values from -10 to 10
- centroids: bfloat16 [8192, 768], P(('col', 'row')), may hold values from -10 to 10
- pattern: int32 [256, 16], P('row'), may hold values from 0 to 63, as said below
Outputs:
- new_centroids: bfloat16 [8192, 768], P(('col', 'row'))
- row_potential: float32 [32768], P('row')
- col_potential: float32 [8192], P('col')
The draws below stay inside these ranges and needn't reach their ends.
Inputs may be any that keep to these rules, and one draw needn't show every extreme that they name: `pattern`: each row lists 16 distinct centroid blocks in rising order; row b always lists block b % 64; every centroid block is listed by some row.
All inputs are finite; a program needn't handle non-finite values.
Results may differ from the reference program's by a relative error of at most 0.0095.
Values may be sent and summed in bfloat16 or wider, within the bound.
A program may use at most 32 MiB of HBM per device.

```python
import math
import jax
import jax.numpy as jnp
from jax import lax

E = 768
ITERS = 3
NCH = 32768
K = 8192
RB = 256
CB = 64
NNZ = 16


def pair_signs(key):
    flips = jax.random.bernoulli(jax.random.fold_in(key, 21), 0.5, (K // 2, E))
    return jnp.where(flips, 1.0, -1.0).astype(jnp.float32)


def lead_magnitude():
    return math.sqrt(16.0 * 170.0 / E)


def centroid_table(key):
    base = jax.random.truncated_normal(jax.random.fold_in(key, 12), -4.0, 4.0, (K, E), jnp.float32)
    signs = jnp.repeat(pair_signs(key), 2, axis=0)
    index = jnp.arange(K, dtype=jnp.int32)
    local = index % 128
    leading = local % 16 == 0
    partner = local % 16 == 1
    magnitude = lead_magnitude()
    table = jnp.where(leading[:, None], magnitude * signs, base)
    table = jnp.where(partner[:, None], 0.99 * magnitude * signs, table)
    return table


def draw_centroids(key, part):
    return centroid_table(key).astype(jnp.bfloat16)


def draw_spans(key, part):
    signs = pair_signs(key)
    values = jax.random.truncated_normal(jax.random.fold_in(key, 15), -4.0, 4.0, (NCH, E), jnp.float32)
    index = jnp.arange(NCH, dtype=jnp.int32)
    target_block = index // 128 % CB
    target = target_block * 128 + 16 * (index * 37 % 8)
    level = index // 61 % 3
    strength = jnp.where(level == 0, 130.0, jnp.where(level == 1, 180.0, 240.0)).astype(jnp.float32)
    amount = strength * 16.0 / (E * lead_magnitude())
    chosen = index % 61 == 0
    aligned = amount[:, None] * signs[target // 2]
    return jnp.where(chosen[:, None], aligned, values).astype(jnp.bfloat16)


def draw_pattern(key, part):
    columns = jnp.arange(CB, dtype=jnp.int32)
    raw_scores = jax.random.randint(jax.random.fold_in(key, 16), (RB, CB), 0, 65536, jnp.int32) * CB + columns[None, :]
    home = jnp.arange(RB, dtype=jnp.int32) % CB
    raw_scores = jnp.where(columns[None, :] == home[:, None], 65536 * CB + CB, raw_scores)
    unused, picked = lax.top_k(raw_scores, NNZ)
    return jnp.sort(picked, axis=1).astype(jnp.int32)


def setup_inputs(seed: int = 0) -> dict:
    splits = jax.random.split(jax.random.key(seed), 4)
    return {
        "spans": draw_spans(jax.random.fold_in(splits[3], 71), 0),
        "centroids": draw_centroids(jax.random.fold_in(splits[3], 71), 0),
        "pattern": draw_pattern(jax.random.fold_in(splits[3], 71), 0),
    }


def reference(spans, centroids, pattern):
    span_blocks = spans.reshape(RB, 128, E)
    centroid_blocks = centroids.reshape(CB, 128, E)

    def block_scores(inputs):
        span_block, listed = inputs
        picked = centroid_blocks[listed]
        return jnp.einsum("ie,nje->nij", span_block.astype(jnp.float32), picked.astype(jnp.float32)) * 0.0625

    scores = lax.map(block_scores, (span_blocks, pattern))
    flat_ids = pattern.reshape(-1)
    col_pot = jnp.zeros((CB, 128), jnp.float32)
    row_pot = jnp.zeros((RB, 128), jnp.float32)
    log_target = jnp.log(jnp.float32(NCH) / jnp.float32(K))
    for sweep in range(ITERS):
        shifted = scores + col_pot[pattern][:, :, None, :]
        row_high = jnp.max(shifted, axis=(1, 3))
        row_sum = jnp.sum(jnp.exp(shifted - row_high[:, None, :, None]), axis=(1, 3))
        row_pot = -(row_high + jnp.log(row_sum))
        shifted = scores + row_pot[:, None, :, None]
        block_high = jnp.max(shifted, axis=2).reshape(-1, 128)
        col_high = jax.ops.segment_max(block_high, flat_ids, num_segments=CB)
        block_sum = jnp.sum(jnp.exp(shifted - col_high[pattern][:, :, None, :]), axis=2).reshape(-1, 128)
        col_sum = jax.ops.segment_sum(block_sum, flat_ids, num_segments=CB)
        col_pot = log_target - (col_high + jnp.log(col_sum))
    plan = jnp.exp(scores + row_pot[:, None, :, None] + col_pot[pattern][:, :, None, :]).astype(jnp.bfloat16)

    def accumulate(running, inputs):
        plan_block, span_block, listed = inputs
        term = jnp.einsum("nij,ie->nje", plan_block.astype(jnp.float32), span_block.astype(jnp.float32))
        return running.at[listed].add(term), None

    start_sum = jnp.zeros((CB, 128, E), jnp.float32)
    summed, unused = lax.scan(accumulate, start_sum, (plan, span_blocks, pattern))
    mass_ratio = jnp.float32(K) / jnp.float32(NCH)
    new_centroids = (summed.reshape(K, E) * mass_ratio).astype(jnp.bfloat16)
    return new_centroids, row_pot.reshape(NCH), col_pot.reshape(K)
```

```python
import functools
import math

import jax
import jax.numpy as jnp
from jax import lax
from jax.experimental import pallas as pl
from jax.experimental.pallas import tpu as pltpu
from jax.sharding import PartitionSpec as P

MESH = pl.DeviceIdType.MESH
FLOOR = -1e30
SCALE = 0.0625
BLOCK = 128
NZ = 32
NXY = 16
STRIDE = 4
NA = NZ // STRIDE
WINDOW = (2, 1, 3)
SPANS, CENT_A, CENT_B, CENT_C = 0, 1, 2, 3
ROW, SIB, COL = 4, 7, 10
HALF, WIN, LAST = 13, 14, 15
NSEM = 16


def remote(src, dst, ssem, rsem, dev):
    return pltpu.make_async_remote_copy(
        src_ref=src, dst_ref=dst, send_sem=ssem, recv_sem=rsem, device_id=dev, device_id_type=MESH
    )


def drain(view, sem):
    pltpu.make_async_copy(view, view, sem).wait()


def kernel(
    log_target, target,
    sp_ref, ce_ref, pat_ref, newc_ref, rp_ref, cp_ref,
    spans_all, cent, plan, acc, half_out, half_in, win_out, win_in, last_out, last_in,
    rowx, sibx, sib_out, colx, total, ssem, rsem,
):
    r, c = lax.axis_index("row"), lax.axis_index("col")
    z, core = r // 2, r % 2
    a, b = z // STRIDE, z % STRIDE
    x, y = c // 4, c % 4
    other = 1 - core
    sibling = (z * 2 + other, c)

    def z_peer(d):
        return (((z + d) % NZ) * 2 + core, c)

    def xy_peer(k):
        return (r, ((x + k // 4) % 4) * 4 + (y + k % 4) % 4)

    def z_step(j):
        return 16 + ((j + 1) // 2) * (1 - 2 * (j % 2))

    def loop(n, fn):
        def step(i, carry):
            fn(i)
            return carry

        lax.fori_loop(0, n, step, 0)

    barrier = pltpu.get_barrier_semaphore()

    def greet(dev):
        pl.semaphore_signal(barrier, inc=1, device_id=dev, device_id_type=MESH)

    loop(NZ - 1, lambda j: greet(z_peer(z_step(j))))
    loop(NXY - 1, lambda j: greet(xy_peer(j + 1)))
    greet(sibling)
    pl.semaphore_wait(barrier, NZ - 1 + NXY - 1 + 1)

    for k in (4, 3, 5, 2, 6, 1, 7):
        remote(ce_ref, cent.at[a, b, core], ssem.at[CENT_A], rsem.at[CENT_A], z_peer(STRIDE * k)).start()
    loop(
        NXY - 1,
        lambda j: remote(
            sp_ref, spans_all.at[c], ssem.at[SPANS], rsem.at[SPANS], xy_peer((10 + j + (j + 10) // 16) % 16)
        ).start(),
    )
    spans_all[c] = sp_ref[...]
    cent[a, b, core] = ce_ref[...]
    drain(cent.at[pl.ds(0, NA - 1), 0, 0], rsem.at[CENT_A])
    for k in WINDOW:
        remote(
            cent.at[:, b, core], cent.at[:, b, core], ssem.at[CENT_B], rsem.at[CENT_B], z_peer(k if k < 3 else NZ - 1)
        ).start()
    drain(cent.at[:, pl.ds(0, 3), 0], rsem.at[CENT_B])
    remote(cent.at[:, :, core], cent.at[:, :, core], ssem.at[CENT_C], rsem.at[CENT_C], sibling).start()
    drain(spans_all.at[pl.ds(0, NXY - 1)], rsem.at[SPANS])
    drain(cent.at[:, :, 0], rsem.at[CENT_C])

    spans = spans_all[...].reshape(NXY * 32, -1)
    table = cent[...].astype(jnp.float32).reshape(NZ * 16, -1).astype(jnp.bfloat16)

    lanes = lax.broadcasted_iota(jnp.int32, (BLOCK, BLOCK), 1)
    diagonal = lax.broadcasted_iota(jnp.int32, (BLOCK, BLOCK), 0) == lanes

    def to_lanes(v):
        return jnp.sum(jnp.where(diagonal, v, 0.0), axis=0, keepdims=True)

    def to_rows(v):
        return jnp.sum(jnp.where(diagonal, v, 0.0), axis=1, keepdims=True)

    def wide(v):
        return jnp.concatenate([v[k : k + 1, :] for k in range(4)], axis=1)

    def rows_of(k):
        return pl.ds(k * BLOCK, BLOCK)

    def row_exchange(n):
        loop(
            NXY - 1,
            lambda j: remote(
                rowx.at[n, c], rowx.at[n, c], ssem.at[ROW + n], rsem.at[ROW + n], xy_peer((10 + j + (j + 10) // 16) % 16)
            ).start(),
        )
        drain(rowx.at[n, pl.ds(0, NXY - 1)], rsem.at[ROW + n])
        return rowx[n]

    def col_exchange_start(n, merge, part):
        for k in range(4):
            sib_out[n, k : k + 1, :] = part[:, k * BLOCK : (k + 1) * BLOCK]
        remote(sib_out.at[n], sibx.at[n], ssem.at[SIB + n], rsem.at[SIB + n], sibling).start()
        drain(sibx.at[n], rsem.at[SIB + n])
        colx[n, z] = merge(jnp.stack([sib_out[n], sibx[n]]))
        loop(
            NZ - 1,
            lambda j: remote(
                colx.at[n, z], colx.at[n, z], ssem.at[COL + n], rsem.at[COL + n], z_peer(z_step(j))
            ).start(),
        )

    def col_exchange_end(n):
        drain(colx.at[n, pl.ds(0, NZ - 1)], rsem.at[COL + n])
        return colx[n]

    def log_sum_exp(v):
        high = jnp.max(v, axis=0)
        return high + jnp.log(jnp.sum(jnp.exp(v - high[None]), axis=0))

    def add_up(v):
        return jnp.sum(v, axis=0)

    for i in range(4):
        listed = pat_ref[i : i + 1, :]
        scores = (
            lax.dot_general(
                spans[i * BLOCK : (i + 1) * BLOCK], table, (((1,), (1,)), ((), ())), preferred_element_type=jnp.float32
            )
            * SCALE
        )
        bias = jnp.concatenate(
            [
                jnp.broadcast_to(
                    jnp.max(jnp.where(listed == c * 4 + k, 0.0, FLOOR), axis=1, keepdims=True), (1, BLOCK)
                )
                for k in range(4)
            ],
            axis=1,
        )
        scores = scores + bias
        plan[rows_of(i), :] = scores
        high = jnp.max(scores, axis=1, keepdims=True)
        rowx[0, c, i : i + 1, :] = to_lanes(high + jnp.log(jnp.sum(jnp.exp(scores - high), axis=1, keepdims=True)))
    row_pot = -log_sum_exp(row_exchange(0))

    high = None
    for i in range(4):
        shifted = plan[rows_of(i), :] + to_rows(row_pot[i : i + 1, :])
        plan[rows_of(i), :] = shifted
        part = jnp.max(shifted, axis=0, keepdims=True)
        high = part if high is None else jnp.maximum(high, part)
    part = jnp.zeros_like(high)
    for i in range(4):
        part = part + jnp.sum(jnp.exp(plan[rows_of(i), :] - high), axis=0, keepdims=True)
    col_exchange_start(0, log_sum_exp, high + jnp.log(part))
    col_pot = log_target - log_sum_exp(col_exchange_end(0))

    for n in (1, 2):
        for i in range(4):
            if n == 1:
                p = jnp.exp(plan[rows_of(i), :] + wide(col_pot))
            else:
                p = plan[rows_of(i), :] * wide(col_scale)
            plan[rows_of(i), :] = p
            rowx[n, c, i : i + 1, :] = to_lanes(jnp.sum(p, axis=1, keepdims=True))
        row_sum = add_up(row_exchange(n))
        row_pot = row_pot - jnp.log(row_sum)
        row_scale = 1.0 / row_sum
        part = None
        for i in range(4):
            p = plan[rows_of(i), :] * to_rows(row_scale[i : i + 1, :])
            plan[rows_of(i), :] = p
            s = jnp.sum(p, axis=0, keepdims=True)
            part = s if part is None else part + s
        col_exchange_start(n, add_up, part)
        if n == 1:
            col_scale = target / add_up(col_exchange_end(n))
            col_pot = col_pot + jnp.log(col_scale)
    rp_ref[...] = row_pot

    sums = lax.dot_general(
        plan[...].astype(jnp.bfloat16), spans, (((0,), (0,)), ((), ())), preferred_element_type=jnp.float32
    )
    acc[...] = sums.reshape(acc.shape)
    half_out[...] = acc[:, :, other].astype(jnp.bfloat16)
    remote(half_out, half_in, ssem.at[HALF], rsem.at[HALF], sibling).start()
    drain(half_in, rsem.at[HALF])
    for s, k in enumerate(WINDOW):
        t = (b + k) % STRIDE
        win_out[s] = (acc[:, t, core] + half_in[:, t].astype(jnp.float32)).astype(jnp.bfloat16)
        remote(
            win_out.at[s], win_in.at[s], ssem.at[WIN], rsem.at[WIN], z_peer(k if k < 3 else NZ - 1)
        ).start()
    group = acc[:, b, core] + half_in[:, b].astype(jnp.float32)
    drain(win_in, rsem.at[WIN])
    for s in range(3):
        group = group + win_in[s].astype(jnp.float32)
    acc[:, b, core] = group
    last_out[...] = group.astype(jnp.bfloat16)
    for k in (4, 3, 5, 2, 6, 1, 7):
        remote(
            last_out.at[(a + k) % NA], last_in.at[k - 1], ssem.at[LAST], rsem.at[LAST], z_peer(STRIDE * k)
        ).start()

    col_sum = add_up(col_exchange_end(2))
    cp_ref[...] = col_pot + jnp.log(target / col_sum)
    total[...] = col_sum
    line = total[pl.ds(z // 8, 1), :]
    place = lax.broadcasted_iota(jnp.int32, (8, BLOCK), 1)
    wanted = lax.broadcasted_iota(jnp.int32, (8, BLOCK), 0) + (z % 8) * 16 + core * 8
    mine = jnp.sum(jnp.where(place == wanted, line, 0.0), axis=1, keepdims=True)

    drain(last_in, rsem.at[LAST])
    out = acc[a, b, core] + jnp.sum(last_in[...].astype(jnp.float32), axis=0)
    newc_ref[...] = (out / mine).astype(jnp.bfloat16)

    drain(spans_all.at[pl.ds(0, NXY - 1)], ssem.at[SPANS])
    drain(cent.at[pl.ds(0, NA - 1), 0, 0], ssem.at[CENT_A])
    drain(cent.at[:, pl.ds(0, 3), 0], ssem.at[CENT_B])
    drain(cent.at[:, :, 0], ssem.at[CENT_C])
    for n in range(3):
        drain(rowx.at[n, pl.ds(0, NXY - 1)], ssem.at[ROW + n])
        drain(sibx.at[n], ssem.at[SIB + n])
        drain(colx.at[n, pl.ds(0, NZ - 1)], ssem.at[COL + n])
    drain(half_in, ssem.at[HALF])
    drain(win_in, ssem.at[WIN])
    drain(last_in, ssem.at[LAST])


def solution(mesh):
    def per_device(spans, centroids, pattern):
        width = spans.shape[1]
        f32, bf16 = jnp.float32, jnp.bfloat16
        target = (spans.shape[0] * mesh.size) / (centroids.shape[0] * mesh.size)
        vmem = pl.BlockSpec(memory_space=pltpu.VMEM)
        new, row_pot, col_pot = pl.pallas_call(
            functools.partial(kernel, math.log(target), target),
            name="sinkhorn",
            out_shape=(
                jax.ShapeDtypeStruct((8, width), bf16),
                jax.ShapeDtypeStruct((4, BLOCK), f32),
                jax.ShapeDtypeStruct((4, BLOCK), f32),
            ),
            in_specs=[vmem] * 3,
            out_specs=(vmem,) * 3,
            scratch_shapes=[
                pltpu.VMEM((NXY, 32, width), bf16),
                pltpu.VMEM((NA, STRIDE, 2, 8, width), bf16),
                pltpu.VMEM((NXY * 32, NZ * 16), f32),
                pltpu.VMEM((NA, STRIDE, 2, 8, width), f32),
                pltpu.VMEM((NA, STRIDE, 8, width), bf16),
                pltpu.VMEM((NA, STRIDE, 8, width), bf16),
                pltpu.VMEM((3, NA, 8, width), bf16),
                pltpu.VMEM((3, NA, 8, width), bf16),
                pltpu.VMEM((NA, 8, width), bf16),
                pltpu.VMEM((NA - 1, 8, width), bf16),
                pltpu.VMEM((3, NXY, 4, BLOCK), f32),
                pltpu.VMEM((3, 4, BLOCK), f32),
                pltpu.VMEM((3, 4, BLOCK), f32),
                pltpu.VMEM((3, NZ, 4, BLOCK), f32),
                pltpu.VMEM((4, BLOCK), f32),
                pltpu.SemaphoreType.DMA((NSEM,)),
                pltpu.SemaphoreType.DMA((NSEM,)),
            ],
            compiler_params=pltpu.CompilerParams(
                collective_id=0, has_side_effects=True, vmem_limit_bytes=32 * 1024 * 1024
            ),
        )(spans, centroids, pattern)
        return new, row_pot.reshape(-1), col_pot.reshape(-1)

    return jax.shard_map(
        per_device,
        mesh=mesh,
        in_specs=(P(("row", "col"), None), P(("col", "row"), None), P("row", None)),
        out_specs=(P(("col", "row"), None), P("row"), P("col")),
        check_vma=False,
    )
```

```python
import functools
import math

import jax
import jax.numpy as jnp
from jax import lax
from jax.experimental import pallas as pl
from jax.experimental.pallas import tpu as pltpu
from jax.sharding import PartitionSpec as P

MESH = pl.DeviceIdType.MESH
FLOOR = -1e30
SCALE = 0.0625
BLOCK = 128
NZ = 32
NXY = 16
STRIDE = 4
NA = NZ // STRIDE
ORDER = (4, 3, 5, 2, 6, 1, 7, 0)
SPANS, CENT_B, CENT_C, CENT_D = 0, 1, 2, 3
ROW, SIB, COL = 4, 7, 10
LAST, UP, DOWN = 13, 14, 18
HALF, WIN = 22, 30
NSEM = 38


def remote(src, dst, ssem, rsem, dev):
    return pltpu.make_async_remote_copy(
        src_ref=src, dst_ref=dst, send_sem=ssem, recv_sem=rsem, device_id=dev, device_id_type=MESH
    )


def drain(view, sem):
    pltpu.make_async_copy(view, view, sem).wait()


def kernel(
    log_target, target,
    sp_ref, ce_ref, pat_ref, newc_ref, rp_ref, cp_ref,
    spans_all, cent, pat, plan, acc, half_out, half_in, win_out, win_in, group, last_out, last_in,
    rowx, sibx, sib_out, colx, total, ssem, rsem, lsem,
):
    r, c = lax.axis_index("row"), lax.axis_index("col")
    z, core = r // 2, r % 2
    a, b = z // STRIDE, z % STRIDE
    x, y = c // 4, c % 4
    other = 1 - core
    sibling = (z * 2 + other, c)

    def z_peer(d):
        return (((z + d) % NZ) * 2 + core, c)

    def xy_peer(k):
        return (r, ((x + k // 4) % 4) * 4 + (y + k % 4) % 4)

    def z_step(j):
        return 16 + ((j + 1) // 2) * (1 - 2 * (j % 2))

    def loop(n, fn):
        def step(i, carry):
            fn(i)
            return carry

        lax.fori_loop(0, n, step, 0)

    local = [
        pltpu.make_async_copy(ce_ref, cent.at[a, b, core], lsem.at[0]),
        pltpu.make_async_copy(sp_ref, spans_all.at[c], lsem.at[1]),
        pltpu.make_async_copy(pat_ref, pat, lsem.at[2]),
    ]
    for copy in local:
        copy.start()

    barrier = pltpu.get_barrier_semaphore()

    def greet(dev):
        pl.semaphore_signal(barrier, inc=1, device_id=dev, device_id_type=MESH)

    for k in (4, 28, 2, 30, 1, 31):
        greet(z_peer(k))
    loop(NXY - 1, lambda j: greet(xy_peer(j + 1)))
    greet(sibling)
    pl.semaphore_wait(barrier, 6 + NXY - 1 + 1)
    for copy in local:
        copy.wait()

    def pass_on(k, onward):
        piece = cent.at[(a - k + NA) % NA, b, core]
        if "up" in onward:
            remote(piece, piece, ssem.at[UP + k], rsem.at[UP + k], z_peer(STRIDE)).start()
        if "down" in onward:
            remote(piece, piece, ssem.at[DOWN - k], rsem.at[DOWN - k], z_peer(NZ - STRIDE)).start()
        for d in (2, 1, 31):
            remote(piece, piece, ssem.at[CENT_B], rsem.at[CENT_B], z_peer(d)).start()

    pass_on(0, ("up", "down"))
    loop(
        NXY - 1,
        lambda j: remote(
            spans_all.at[c], spans_all.at[c], ssem.at[SPANS], rsem.at[SPANS], xy_peer((10 + j + (j + 10) // 16) % 16)
        ).start(),
    )
    for k in (1, 2, 3, 4):
        drain(cent.at[0, 0, 0], rsem.at[UP + k - 1])
        pass_on(k, ("up",) if k < 4 else ())
        if k < 4:
            drain(cent.at[0, 0, 0], rsem.at[DOWN + k - 1])
            pass_on(-k, ("down",) if k < 3 else ())
    remote(cent.at[:, b, core], cent.at[:, b, core], ssem.at[CENT_C], rsem.at[CENT_C], sibling).start()
    drain(cent.at[:, pl.ds(0, 3), 0], rsem.at[CENT_B])
    for k in (1, 2, 3):
        t = (b + k) % STRIDE
        remote(cent.at[:, t, core], cent.at[:, t, core], ssem.at[CENT_D], rsem.at[CENT_D], sibling).start()
    drain(spans_all.at[pl.ds(0, NXY - 1)], rsem.at[SPANS])
    drain(cent.at[:, 0, 0], rsem.at[CENT_C])
    drain(cent.at[:, pl.ds(0, 3), 0], rsem.at[CENT_D])

    spans = spans_all[...].reshape(NXY * 32, -1)
    table = cent[...].astype(jnp.float32).reshape(NZ * 16, -1).astype(jnp.bfloat16)

    lanes = lax.broadcasted_iota(jnp.int32, (BLOCK, BLOCK), 1)
    diagonal = lax.broadcasted_iota(jnp.int32, (BLOCK, BLOCK), 0) == lanes

    def to_lanes(v):
        return jnp.sum(jnp.where(diagonal, v, 0.0), axis=0, keepdims=True)

    def to_rows(v):
        return jnp.sum(jnp.where(diagonal, v, 0.0), axis=1, keepdims=True)

    def wide(v):
        return jnp.concatenate([v[k : k + 1, :] for k in range(4)], axis=1)

    def rows_of(k):
        return pl.ds(k * BLOCK, BLOCK)

    def row_exchange(n):
        loop(
            NXY - 1,
            lambda j: remote(
                rowx.at[n, c], rowx.at[n, c], ssem.at[ROW + n], rsem.at[ROW + n], xy_peer((10 + j + (j + 10) // 16) % 16)
            ).start(),
        )
        drain(rowx.at[n, pl.ds(0, NXY - 1)], rsem.at[ROW + n])
        return rowx[n]

    def sibling_send(n, part):
        for k in range(4):
            sib_out[n, k : k + 1, :] = part[:, k * BLOCK : (k + 1) * BLOCK]
        remote(sib_out.at[n], sibx.at[n], ssem.at[SIB + n], rsem.at[SIB + n], sibling).start()

    def col_send(n, merge):
        drain(sibx.at[n], rsem.at[SIB + n])
        colx[n, z] = merge(jnp.stack([sib_out[n], sibx[n]]))
        loop(
            NZ - 1,
            lambda j: remote(
                colx.at[n, z], colx.at[n, z], ssem.at[COL + n], rsem.at[COL + n], z_peer(z_step(j))
            ).start(),
        )

    def col_exchange_end(n):
        drain(colx.at[n, pl.ds(0, NZ - 1)], rsem.at[COL + n])
        return colx[n]

    def log_sum_exp(v):
        high = jnp.max(v, axis=0)
        return high + jnp.log(jnp.sum(jnp.exp(v - high[None]), axis=0))

    def add_up(v):
        return jnp.sum(v, axis=0)

    for i in range(4):
        listed = pat[i : i + 1, :]
        scores = (
            lax.dot_general(
                spans[i * BLOCK : (i + 1) * BLOCK], table, (((1,), (1,)), ((), ())), preferred_element_type=jnp.float32
            )
            * SCALE
        )
        bias = jnp.concatenate(
            [
                jnp.broadcast_to(
                    jnp.max(jnp.where(listed == c * 4 + k, 0.0, FLOOR), axis=1, keepdims=True), (1, BLOCK)
                )
                for k in range(4)
            ],
            axis=1,
        )
        scores = scores + bias
        plan[rows_of(i), :] = scores
        high = jnp.max(scores, axis=1, keepdims=True)
        rowx[0, c, i : i + 1, :] = to_lanes(high + jnp.log(jnp.sum(jnp.exp(scores - high), axis=1, keepdims=True)))
    row_pot = -log_sum_exp(row_exchange(0))

    high = None
    for i in range(4):
        shifted = plan[rows_of(i), :] + to_rows(row_pot[i : i + 1, :])
        plan[rows_of(i), :] = shifted
        part = jnp.max(shifted, axis=0, keepdims=True)
        high = part if high is None else jnp.maximum(high, part)
    part = jnp.zeros_like(high)
    for i in range(4):
        part = part + jnp.sum(jnp.exp(plan[rows_of(i), :] - high), axis=0, keepdims=True)
    sibling_send(0, high + jnp.log(part))
    col_send(0, log_sum_exp)
    col_pot = log_target - log_sum_exp(col_exchange_end(0))

    for n in (1, 2):
        for i in range(4):
            if n == 1:
                p = jnp.exp(plan[rows_of(i), :] + wide(col_pot))
            else:
                p = plan[rows_of(i), :] * wide(col_scale)
            plan[rows_of(i), :] = p
            rowx[n, c, i : i + 1, :] = to_lanes(jnp.sum(p, axis=1, keepdims=True))
        row_sum = add_up(row_exchange(n))
        row_pot = row_pot - jnp.log(row_sum)
        row_scale = 1.0 / row_sum
        part = None
        for i in range(4):
            p = plan[rows_of(i), :] * to_rows(row_scale[i : i + 1, :])
            plan[rows_of(i), :] = p
            s = jnp.sum(p, axis=0, keepdims=True)
            part = s if part is None else part + s
        sibling_send(n, part)
        if n == 1:
            col_send(n, add_up)
            col_scale = target / add_up(col_exchange_end(n))
            col_pot = col_pot + jnp.log(col_scale)
    rp_ref[...] = row_pot

    sums = lax.dot_general(
        plan[...].astype(jnp.bfloat16), spans, (((0,), (0,)), ((), ())), preferred_element_type=jnp.float32
    )
    acc[...] = sums.reshape(acc.shape)

    def stop(d):
        q = (z + d) % NZ
        return q // STRIDE, q % STRIDE

    stops = [stop(d) for d in (2, 1, 31)] + [(a, b)]
    for i, k in enumerate(ORDER):
        for s, (qa, qb) in enumerate(stops):
            half_out[i, s] = acc[(qa + k) % NA, qb, other].astype(jnp.bfloat16)
        remote(half_out.at[i], half_in.at[i], ssem.at[HALF + i], rsem.at[HALF + i], sibling).start()
    for i, k in enumerate(ORDER):
        drain(half_in.at[i], rsem.at[HALF + i])
        for s, (qa, qb) in enumerate(stops):
            both = acc[(qa + k) % NA, qb, core] + half_in[i, s].astype(jnp.float32)
            if s == 3:
                group[i] = both
                continue
            win_out[i, s] = both.astype(jnp.bfloat16)
            remote(
                win_out.at[i, s], win_in.at[i, s], ssem.at[WIN + i], rsem.at[WIN + i], z_peer((2, 1, 31)[s])
            ).start()
    col_send(2, add_up)
    for i, k in enumerate(ORDER):
        drain(win_in.at[i], rsem.at[WIN + i])
        whole = group[i]
        for s in range(3):
            whole = whole + win_in[i, s].astype(jnp.float32)
        if k == 0:
            group[i] = whole
            continue
        last_out[i] = whole.astype(jnp.bfloat16)
        remote(last_out.at[i], last_in.at[i], ssem.at[LAST], rsem.at[LAST], z_peer(STRIDE * k)).start()

    col_sum = add_up(col_exchange_end(2))
    cp_ref[...] = col_pot + jnp.log(target / col_sum)
    total[...] = col_sum
    line = total[pl.ds(z // 8, 1), :]
    place = lax.broadcasted_iota(jnp.int32, (8, BLOCK), 1)
    wanted = lax.broadcasted_iota(jnp.int32, (8, BLOCK), 0) + (z % 8) * 16 + core * 8
    mine = jnp.sum(jnp.where(place == wanted, line, 0.0), axis=1, keepdims=True)

    drain(last_in, rsem.at[LAST])
    out = group[NA - 1] + jnp.sum(last_in[...].astype(jnp.float32), axis=0)
    newc_ref[...] = (out / mine).astype(jnp.bfloat16)

    drain(spans_all.at[pl.ds(0, NXY - 1)], ssem.at[SPANS])
    drain(cent.at[:, pl.ds(0, 3), 0], ssem.at[CENT_B])
    drain(cent.at[:, 0, 0], ssem.at[CENT_C])
    drain(cent.at[:, pl.ds(0, 3), 0], ssem.at[CENT_D])
    for k in range(4):
        drain(cent.at[0, 0, 0], ssem.at[UP + k])
    for k in range(3):
        drain(cent.at[0, 0, 0], ssem.at[DOWN + k])
    for n in range(3):
        drain(rowx.at[n, pl.ds(0, NXY - 1)], ssem.at[ROW + n])
        drain(sibx.at[n], ssem.at[SIB + n])
        drain(colx.at[n, pl.ds(0, NZ - 1)], ssem.at[COL + n])
    for i in range(NA):
        drain(half_in.at[i], ssem.at[HALF + i])
        drain(win_in.at[i], ssem.at[WIN + i])
    drain(last_in, ssem.at[LAST])


def solution(mesh):
    def per_device(spans, centroids, pattern):
        width = spans.shape[1]
        f32, bf16 = jnp.float32, jnp.bfloat16
        target = (spans.shape[0] * mesh.size) / (centroids.shape[0] * mesh.size)
        vmem = pl.BlockSpec(memory_space=pltpu.VMEM)
        new, row_pot, col_pot = pl.pallas_call(
            functools.partial(kernel, math.log(target), target),
            name="sinkhorn",
            out_shape=(
                jax.ShapeDtypeStruct((8, width), bf16),
                jax.ShapeDtypeStruct((4, BLOCK), f32),
                jax.ShapeDtypeStruct((4, BLOCK), f32),
            ),
            in_specs=[pl.BlockSpec(memory_space=pltpu.HBM)] * 3,
            out_specs=(vmem,) * 3,
            scratch_shapes=[
                pltpu.VMEM((NXY, 32, width), bf16),
                pltpu.VMEM((NA, STRIDE, 2, 8, width), bf16),
                pltpu.VMEM((4, 16), jnp.int32),
                pltpu.VMEM((NXY * 32, NZ * 16), f32),
                pltpu.VMEM((NA, STRIDE, 2, 8, width), f32),
                pltpu.VMEM((NA, 4, 8, width), bf16),
                pltpu.VMEM((NA, 4, 8, width), bf16),
                pltpu.VMEM((NA, 3, 8, width), bf16),
                pltpu.VMEM((NA, 3, 8, width), bf16),
                pltpu.VMEM((NA, 8, width), f32),
                pltpu.VMEM((NA - 1, 8, width), bf16),
                pltpu.VMEM((NA - 1, 8, width), bf16),
                pltpu.VMEM((3, NXY, 4, BLOCK), f32),
                pltpu.VMEM((3, 4, BLOCK), f32),
                pltpu.VMEM((3, 4, BLOCK), f32),
                pltpu.VMEM((3, NZ, 4, BLOCK), f32),
                pltpu.VMEM((4, BLOCK), f32),
                pltpu.SemaphoreType.DMA((NSEM,)),
                pltpu.SemaphoreType.DMA((NSEM,)),
                pltpu.SemaphoreType.DMA((3,)),
            ],
            compiler_params=pltpu.CompilerParams(
                collective_id=0, has_side_effects=True, vmem_limit_bytes=32 * 1024 * 1024
            ),
        )(spans, centroids, pattern)
        return new, row_pot.reshape(-1), col_pot.reshape(-1)

    return jax.shard_map(
        per_device,
        mesh=mesh,
        in_specs=(P(("row", "col"), None), P(("col", "row"), None), P("row", None)),
        out_specs=(P(("col", "row"), None), P("row"), P("col")),
        check_vma=False,
    )
```

```python
import functools
import math

import jax
import jax.numpy as jnp
from jax import lax
from jax.experimental import pallas as pl
from jax.experimental.pallas import tpu as pltpu
from jax.sharding import PartitionSpec as P

MESH = pl.DeviceIdType.MESH
FLOOR = -1e30
SCALE = 0.0625
BLOCK = 128
NZ = 32
NXY = 16
STRIDE = 4
NA = NZ // STRIDE
SPREAD = {0: (2, -2, 1, -1), 1: (2, 1, -1), -1: (-2, 1, -1), 2: (2, 1, -1), -2: (-2, 1, -1), 3: (3, 2, 1, -1), -3: (-3, -2, 1, -1), 4: ()}
ORDER = (4, 3, -3, 2, -2, 1, -1, 0)
WINDOW = [(k, d) for k in ORDER for d in SPREAD[k]]
SPANS, OTHER, PAT, CENT, POT, LAST = range(6)
ROW, COL, STOP, WIN = 6, 9, 12, 19
NSEM = 27


def remote(src, dst, ssem, rsem, dev):
    return pltpu.make_async_remote_copy(
        src_ref=src, dst_ref=dst, send_sem=ssem, recv_sem=rsem, device_id=dev, device_id_type=MESH
    )


def drain(view, sem):
    pltpu.make_async_copy(view, view, sem).wait()


def kernel(
    log_target, target,
    sp_ref, ce_ref, pat_ref, newc_ref, rp_ref, cp_ref,
    spans_all, cent, pat, plan, acc, win_out, win_in, last_out, last_in, rowx, colx, pots, total, ssem, rsem, lsem,
):
    r, c = lax.axis_index("row"), lax.axis_index("col")
    z, core = r // 2, r % 2
    a, b = z // STRIDE, z % STRIDE
    x, y = c // 4, c % 4
    other = 1 - core
    sibling = (z * 2 + other, c)

    def z_peer(d):
        return (((z + d + NZ) % NZ) * 2 + core, c)

    def far_first(i):
        return (2 + ((i + 1) // 2) * (1 - 2 * (i % 2))) % 4

    def xy_peer(j, flip):
        return (z * 2 + (core + flip) % 2, ((x + far_first(j // 4)) % 4) * 4 + (y + far_first(j % 4)) % 4)

    def z_step(j):
        return 16 + ((j + 1) // 2) * (1 - 2 * (j % 2))

    def loop(n, fn):
        def step(i, carry):
            fn(i)
            return carry

        lax.fori_loop(0, n, step, 0)

    local = [
        pltpu.make_async_copy(ce_ref, cent.at[a, b], lsem.at[0]),
        pltpu.make_async_copy(sp_ref, spans_all.at[core, c], lsem.at[1]),
        pltpu.make_async_copy(pat_ref, pat.at[core], lsem.at[2]),
    ]
    for copy in local:
        copy.start()

    barrier = pltpu.get_barrier_semaphore()

    def greet(dev):
        pl.semaphore_signal(barrier, inc=1, device_id=dev, device_id_type=MESH)

    near = [d * s for d in (8, 4, 3, 2, 1) for s in (1, -1)]
    for d in near:
        greet(z_peer(d))
    loop(NXY - 1, lambda j: greet(xy_peer(j, 0)))
    greet(sibling)
    pl.semaphore_wait(barrier, len(near) + NXY - 1 + 1)
    for copy in local:
        copy.wait()

    def chunk(k):
        return cent.at[(a - k + NA) % NA, b]

    def go(k, d, n):
        remote(chunk(k), chunk(k), ssem.at[STOP + n], rsem.at[STOP + n], z_peer(STRIDE * d)).start()

    def come(n):
        drain(chunk(0), rsem.at[STOP + n])

    def spread(k):
        for d in SPREAD[k]:
            remote(chunk(k), chunk(k), ssem.at[CENT], rsem.at[CENT], z_peer(d)).start()

    go(0, 2, 2)
    go(0, -2, 3)
    go(0, 1, 0)
    go(0, -1, 1)
    spread(0)
    mine = spans_all.at[core, c]
    loop(NXY - 1, lambda j: remote(mine, mine, ssem.at[SPANS], rsem.at[SPANS], xy_peer(j, 0)).start())
    remote(pat.at[core], pat.at[core], ssem.at[PAT], rsem.at[PAT], sibling).start()
    come(0)
    spread(1)
    come(1)
    spread(-1)
    come(2)
    go(2, 1, 4)
    come(3)
    go(-2, -1, 5)
    go(2 - 4 * core, 2 - 4 * core, 6)
    spread(2)
    spread(-2)
    drain(spans_all.at[0, pl.ds(0, NXY - 1)], rsem.at[SPANS])
    remote(spans_all.at[core], spans_all.at[core], ssem.at[OTHER], rsem.at[OTHER], sibling).start()
    come(4)
    spread(3)
    come(5)
    spread(-3)
    come(6)
    drain(pat.at[0], rsem.at[PAT])
    drain(spans_all.at[0], rsem.at[OTHER])
    drain(cent.at[:, pl.ds(0, 3)], rsem.at[CENT])

    spans = spans_all[...].reshape(2 * NXY * 32, -1)
    table = cent[...].astype(jnp.float32).reshape(NZ * 8, -1).astype(jnp.bfloat16)
    nblocks = 8

    down = lax.broadcasted_iota(jnp.int32, (BLOCK, BLOCK), 0)
    lanes = lax.broadcasted_iota(jnp.int32, (BLOCK, BLOCK), 1)
    diagonal = down == lanes

    def to_lanes(v):
        return jnp.sum(jnp.where(diagonal, v, 0.0), axis=0, keepdims=True)

    def to_rows(v):
        return jnp.sum(jnp.where(diagonal, v, 0.0), axis=1, keepdims=True)

    def wide(v):
        return jnp.concatenate([v[0:1, :], v[1:2, :]], axis=1)

    def rows_of(k):
        return pl.ds(k * BLOCK, BLOCK)

    me = c * 2 + core

    def row_exchange(n):
        part = rowx.at[n, me]
        loop(
            2 * (NXY - 1),
            lambda j: remote(part, part, ssem.at[ROW + n], rsem.at[ROW + n], xy_peer(j // 2, j % 2)).start(),
        )
        remote(part, part, ssem.at[ROW + n], rsem.at[ROW + n], sibling).start()
        drain(rowx.at[n, pl.ds(0, 2 * NXY - 1)], rsem.at[ROW + n])
        return rowx[n]

    def col_send(n, part):
        colx[n, z, 0:1, :] = part[:, :BLOCK]
        colx[n, z, 1:2, :] = part[:, BLOCK:]
        piece = colx.at[n, z]
        loop(NZ - 1, lambda j: remote(piece, piece, ssem.at[COL + n], rsem.at[COL + n], z_peer(z_step(j))).start())

    def col_receive(n):
        drain(colx.at[n, pl.ds(0, NZ - 1)], rsem.at[COL + n])
        return colx[n]

    def log_sum_exp(v):
        high = jnp.max(v, axis=0)
        return high + jnp.log(jnp.sum(jnp.exp(v - high[None]), axis=0))

    def add_up(v):
        return jnp.sum(v, axis=0)

    block_of = lax.broadcasted_iota(jnp.int32, (1, NZ * 8), 1) // 64
    for i in range(nblocks):
        listed = pat[i // 4, i % 4 : i % 4 + 1, :]
        bias = jnp.zeros((1, NZ * 8), jnp.float32)
        for k in range(4):
            cell = jnp.max(jnp.where(listed == c * 4 + k, 0.0, FLOOR), axis=1, keepdims=True)
            bias = bias + jnp.where(block_of == k, cell, 0.0)
        scores = (
            lax.dot_general(
                spans[i * BLOCK : (i + 1) * BLOCK], table, (((1,), (1,)), ((), ())), preferred_element_type=jnp.float32
            )
            * SCALE
            + bias
        )
        plan[rows_of(i), :] = scores
        high = jnp.max(scores, axis=1, keepdims=True)
        rowx[0, me, i : i + 1, :] = to_lanes(high + jnp.log(jnp.sum(jnp.exp(scores - high), axis=1, keepdims=True)))
    row_pot = -log_sum_exp(row_exchange(0))

    high = None
    for i in range(nblocks):
        shifted = plan[rows_of(i), :] + to_rows(row_pot[i : i + 1, :])
        plan[rows_of(i), :] = shifted
        part = jnp.max(shifted, axis=0, keepdims=True)
        high = part if high is None else jnp.maximum(high, part)
    part = jnp.zeros_like(high)
    for i in range(nblocks):
        part = part + jnp.sum(jnp.exp(plan[rows_of(i), :] - high), axis=0, keepdims=True)
    col_send(0, high + jnp.log(part))
    col_pot = log_target - log_sum_exp(col_receive(0))

    for n in (1, 2):
        for i in range(nblocks):
            if n == 1:
                p = jnp.exp(plan[rows_of(i), :] + wide(col_pot))
            else:
                p = plan[rows_of(i), :] * wide(col_scale)
            plan[rows_of(i), :] = p
            rowx[n, me, i : i + 1, :] = to_lanes(jnp.sum(p, axis=1, keepdims=True))
        row_sum = add_up(row_exchange(n))
        row_pot = row_pot - jnp.log(row_sum)
        row_scale = 1.0 / row_sum
        part = None
        for i in range(nblocks):
            p = plan[rows_of(i), :] * to_rows(row_scale[i : i + 1, :])
            plan[rows_of(i), :] = p
            s = jnp.sum(p, axis=0, keepdims=True)
            part = s if part is None else part + s
        if n == 1:
            col_send(n, part)
            col_scale = target / add_up(col_receive(n))
            col_pot = col_pot + jnp.log(col_scale)

    sums = lax.dot_general(
        plan[...].astype(jnp.bfloat16), spans, (((0,), (0,)), ((), ())), preferred_element_type=jnp.float32
    )
    acc[...] = sums.reshape(acc.shape)

    def send_last(i, k, whole):
        last_out[i] = whole.astype(jnp.bfloat16)
        remote(last_out.at[i], last_in.at[i], ssem.at[LAST], rsem.at[LAST], z_peer(-STRIDE * k)).start()

    send_last(0, 4, acc[(a + 4) % NA, b])
    for w, (k, d) in enumerate(WINDOW):
        stop = (z - d + NZ) % NZ
        win_out[w] = acc[(stop // STRIDE - k + NA) % NA, stop % STRIDE].astype(jnp.bfloat16)
        sem = WIN + ORDER.index(k)
        remote(win_out.at[w], win_in.at[w], ssem.at[sem], rsem.at[sem], z_peer(-d)).start()
    col_send(2, part)
    for i, k in enumerate(ORDER):
        if k == 4:
            continue
        lo = [w for w, (q, _) in enumerate(WINDOW) if q == k][0]
        drain(win_in.at[pl.ds(lo, len(SPREAD[k]))], rsem.at[WIN + i])
        whole = acc[(a - k + NA) % NA, b]
        for w in range(lo, lo + len(SPREAD[k])):
            whole = whole + win_in[w].astype(jnp.float32)
        if k != 0:
            send_last(i, k, whole)

    rp_ref[...] = jnp.where(core == 0, row_pot[:4, :], row_pot[4:, :])
    col_sum = add_up(col_receive(2))
    pots[core] = col_pot + jnp.log(target / col_sum)
    remote(pots.at[core], pots.at[core], ssem.at[POT], rsem.at[POT], sibling).start()
    total[...] = col_sum
    line = total[pl.ds(z // 16, 1), :]
    wanted = lax.broadcasted_iota(jnp.int32, (8, BLOCK), 0) + (z % 16) * 8
    place = lax.broadcasted_iota(jnp.int32, (8, BLOCK), 1)
    mass = jnp.sum(jnp.where(place == wanted, line, 0.0), axis=1, keepdims=True)
    drain(pots.at[0], rsem.at[POT])
    for i in range(4):
        line = jnp.zeros((1, BLOCK), jnp.float32)
        for q in range(2):
            take = (down == (i % 2) * 64 + (lanes // 16) * 8 + lanes % 8) & (lanes // 8 % 2 == q)
            line = line + jnp.sum(jnp.where(take, to_rows(pots[q, i // 2 : i // 2 + 1, :]), 0.0), axis=0, keepdims=True)
        cp_ref[i : i + 1, :] = line

    drain(last_in, rsem.at[LAST])
    out = whole + jnp.sum(last_in[...].astype(jnp.float32), axis=0)
    newc_ref[...] = (out / mass).astype(jnp.bfloat16)

    drain(spans_all.at[0, pl.ds(0, NXY - 1)], ssem.at[SPANS])
    drain(spans_all.at[0], ssem.at[OTHER])
    drain(pat.at[0], ssem.at[PAT])
    drain(cent.at[:, pl.ds(0, 3)], ssem.at[CENT])
    for n in range(7):
        drain(chunk(0), ssem.at[STOP + n])
    for n in range(3):
        drain(rowx.at[n, pl.ds(0, 2 * NXY - 1)], ssem.at[ROW + n])
        drain(colx.at[n, pl.ds(0, NZ - 1)], ssem.at[COL + n])
    for i, k in enumerate(ORDER):
        if k != 4:
            drain(win_in.at[pl.ds(0, len(SPREAD[k]))], ssem.at[WIN + i])
    drain(pots.at[0], ssem.at[POT])
    drain(last_in, ssem.at[LAST])


def solution(mesh):
    def per_device(spans, centroids, pattern):
        width = spans.shape[1]
        f32, bf16 = jnp.float32, jnp.bfloat16
        target = (spans.shape[0] * mesh.size) / (centroids.shape[0] * mesh.size)
        args = [pltpu.with_memory_space_constraint(v, pltpu.HBM) for v in (spans, centroids, pattern)]
        vmem = pl.BlockSpec(memory_space=pltpu.VMEM)
        new, row_pot, col_pot = pl.pallas_call(
            functools.partial(kernel, math.log(target), target),
            name="sinkhorn",
            out_shape=(
                jax.ShapeDtypeStruct((8, width), bf16),
                jax.ShapeDtypeStruct((4, BLOCK), f32),
                jax.ShapeDtypeStruct((4, BLOCK), f32),
            ),
            in_specs=[pl.BlockSpec(memory_space=pltpu.HBM)] * 3,
            out_specs=(vmem,) * 3,
            scratch_shapes=[
                pltpu.VMEM((2, NXY, 32, width), bf16),
                pltpu.VMEM((NA, STRIDE, 8, width), bf16),
                pltpu.VMEM((2, 4, 16), jnp.int32),
                pltpu.VMEM((2 * NXY * 32, NZ * 8), f32),
                pltpu.VMEM((NA, STRIDE, 8, width), f32),
                pltpu.VMEM((len(WINDOW), 8, width), bf16),
                pltpu.VMEM((len(WINDOW), 8, width), bf16),
                pltpu.VMEM((NA - 1, 8, width), bf16),
                pltpu.VMEM((NA - 1, 8, width), bf16),
                pltpu.VMEM((3, 2 * NXY, 8, BLOCK), f32),
                pltpu.VMEM((3, NZ, 2, BLOCK), f32),
                pltpu.VMEM((2, 2, BLOCK), f32),
                pltpu.VMEM((2, BLOCK), f32),
                pltpu.SemaphoreType.DMA((NSEM,)),
                pltpu.SemaphoreType.DMA((NSEM,)),
                pltpu.SemaphoreType.DMA((3,)),
            ],
            compiler_params=pltpu.CompilerParams(
                collective_id=0, has_side_effects=True, vmem_limit_bytes=32 * 1024 * 1024
            ),
        )(*args)
        return new, row_pot.reshape(-1), col_pot.reshape(-1)

    return jax.shard_map(
        per_device,
        mesh=mesh,
        in_specs=(P(("row", "col"), None), P(("col", "row"), None), P("row", None)),
        out_specs=(P(("col", "row"), None), P("row"), P("col")),
        check_vma=False,
    )
```

```python
import functools
import math

import jax
import jax.numpy as jnp
from jax import lax
from jax.experimental import pallas as pl
from jax.experimental.pallas import tpu as pltpu
from jax.sharding import PartitionSpec as P

MESH = pl.DeviceIdType.MESH
FLOOR = -1e30
SCALE = 0.0625
BLOCK = 128
NZ = 32
NXY = 16
STRIDE = 4
NA = NZ // STRIDE
SPREAD = {0: (2, -2, 1, -1), 1: (2, 1, -1), -1: (-2, 1, -1), 2: (2, 1, -1), -2: (-2, 1, -1), 3: (3, 2, 1, -1), -3: (-3, -2, 1, -1), 4: ()}
ORDER = (4, 3, -3, 2, -2, 1, -1, 0)
WINDOW = [(k, d) for k in ORDER for d in SPREAD[k]]
SPANS, OTHER, PAT, CENT, POT, LAST = range(6)
ROW, COL, STOP, WIN = 6, 9, 12, 19
NSEM = 27


def remote(src, dst, ssem, rsem, dev):
    return pltpu.make_async_remote_copy(
        src_ref=src, dst_ref=dst, send_sem=ssem, recv_sem=rsem, device_id=dev, device_id_type=MESH
    )


def drain(view, sem):
    pltpu.make_async_copy(view, view, sem).wait()


def kernel(
    log_target, target,
    sp_ref, ce_ref, pat_ref, newc_ref, rp_ref, cp_ref,
    spans_all, cent, pat, plan, acc, win_out, win_in, last_out, last_in, rowx, colx, pots, total, ssem, rsem, lsem, hsem,
):
    r, c = lax.axis_index("row"), lax.axis_index("col")
    z, core = r // 2, r % 2
    a, b = z // STRIDE, z % STRIDE
    x, y = c // 4, c % 4
    other = 1 - core
    sibling = (z * 2 + other, c)

    def z_peer(d):
        return (((z + d + NZ) % NZ) * 2 + core, c)

    def far_first(i):
        return (2 + ((i + 1) // 2) * (1 - 2 * (i % 2))) % 4

    def xy_peer(j, flip):
        return (z * 2 + (core + flip) % 2, ((x + far_first(j // 4)) % 4) * 4 + (y + far_first(j % 4)) % 4)

    def z_step(j):
        return 16 + ((j + 1) // 2) * (1 - 2 * (j % 2))

    def loop(n, fn):
        def step(i, carry):
            fn(i)
            return carry

        lax.fori_loop(0, n, step, 0)

    local = [
        pltpu.make_async_copy(ce_ref, cent.at[a, b], lsem.at[0]),
        pltpu.make_async_copy(sp_ref, spans_all.at[core, c], lsem.at[1]),
        pltpu.make_async_copy(pat_ref, pat.at[core], lsem.at[2]),
    ]
    for copy in local:
        copy.start()

    barrier = pltpu.get_barrier_semaphore()

    def greet(dev):
        pl.semaphore_signal(barrier, inc=1, device_id=dev, device_id_type=MESH)

    near = [d * s for d in (4, 3, 2, 1) for s in (1, -1)]
    for d in near:
        greet(z_peer(d))
    loop(NXY - 1, lambda j: greet(xy_peer(j, 0)))
    greet(sibling)
    pl.semaphore_wait(barrier, len(near) + NXY - 1 + 1)
    for d in (STRIDE, -STRIDE):
        pl.semaphore_signal(hsem, inc=1, device_id=z_peer(d), device_id_type=MESH)
    for copy in local:
        copy.wait()

    def chunk(k):
        return cent.at[(a - k + NA) % NA, b]

    def go(k, d, n):
        remote(chunk(k), chunk(k), ssem.at[STOP + n], rsem.at[STOP + n], z_peer(STRIDE * d)).start()

    def come(n):
        drain(chunk(0), rsem.at[STOP + n])

    def spread(k):
        for d in SPREAD[k]:
            remote(chunk(k), chunk(k), ssem.at[CENT], rsem.at[CENT], z_peer(d)).start()

    go(0, 1, 0)
    go(0, -1, 1)
    spread(0)
    mine = spans_all.at[core, c]
    loop(NXY - 1, lambda j: remote(mine, mine, ssem.at[SPANS], rsem.at[SPANS], xy_peer(j, 0)).start())
    remote(pat.at[core], pat.at[core], ssem.at[PAT], rsem.at[PAT], sibling).start()
    pl.semaphore_wait(hsem, 2)
    come(0)
    go(1, 2, 4)
    go(1, 1, 2)
    spread(1)
    come(1)
    go(-1, -2, 5)
    go(-1, -1, 3)
    spread(-1)
    come(2)
    spread(2)
    come(3)
    spread(-2)
    drain(spans_all.at[0, pl.ds(0, NXY - 1)], rsem.at[SPANS])
    remote(spans_all.at[core], spans_all.at[core], ssem.at[OTHER], rsem.at[OTHER], sibling).start()
    come(4)
    come(5)
    go(3 - 6 * core, 1 - 2 * core, 6)
    spread(3)
    spread(-3)
    come(6)
    drain(pat.at[0], rsem.at[PAT])
    drain(spans_all.at[0], rsem.at[OTHER])
    drain(cent.at[:, pl.ds(0, 3)], rsem.at[CENT])

    spans = spans_all[...].reshape(2 * NXY * 32, -1)
    table = cent[...].astype(jnp.float32).reshape(NZ * 8, -1).astype(jnp.bfloat16)
    nblocks = 8

    down = lax.broadcasted_iota(jnp.int32, (BLOCK, BLOCK), 0)
    lanes = lax.broadcasted_iota(jnp.int32, (BLOCK, BLOCK), 1)
    diagonal = down == lanes

    def to_lanes(v):
        return jnp.sum(jnp.where(diagonal, v, 0.0), axis=0, keepdims=True)

    def to_rows(v):
        return jnp.sum(jnp.where(diagonal, v, 0.0), axis=1, keepdims=True)

    def wide(v):
        return jnp.concatenate([v[0:1, :], v[1:2, :]], axis=1)

    def rows_of(k):
        return pl.ds(k * BLOCK, BLOCK)

    me = c * 2 + core

    def row_exchange(n):
        part = rowx.at[n, me]
        loop(
            2 * (NXY - 1),
            lambda j: remote(part, part, ssem.at[ROW + n], rsem.at[ROW + n], xy_peer(j // 2, j % 2)).start(),
        )
        remote(part, part, ssem.at[ROW + n], rsem.at[ROW + n], sibling).start()
        drain(rowx.at[n, pl.ds(0, 2 * NXY - 1)], rsem.at[ROW + n])
        return rowx[n]

    def col_send(n, part):
        colx[n, z, 0:1, :] = part[:, :BLOCK]
        colx[n, z, 1:2, :] = part[:, BLOCK:]
        piece = colx.at[n, z]
        loop(NZ - 1, lambda j: remote(piece, piece, ssem.at[COL + n], rsem.at[COL + n], z_peer(z_step(j))).start())

    def col_receive(n):
        drain(colx.at[n, pl.ds(0, NZ - 1)], rsem.at[COL + n])
        return colx[n]

    def log_sum_exp(v):
        high = jnp.max(v, axis=0)
        return high + jnp.log(jnp.sum(jnp.exp(v - high[None]), axis=0))

    def add_up(v):
        return jnp.sum(v, axis=0)

    block_of = lax.broadcasted_iota(jnp.int32, (1, NZ * 8), 1) // 64
    for i in range(nblocks):
        listed = pat[i // 4, i % 4 : i % 4 + 1, :]
        bias = jnp.zeros((1, NZ * 8), jnp.float32)
        for k in range(4):
            cell = jnp.max(jnp.where(listed == c * 4 + k, 0.0, FLOOR), axis=1, keepdims=True)
            bias = bias + jnp.where(block_of == k, cell, 0.0)
        scores = (
            lax.dot_general(
                spans[i * BLOCK : (i + 1) * BLOCK], table, (((1,), (1,)), ((), ())), preferred_element_type=jnp.float32
            )
            * SCALE
            + bias
        )
        plan[rows_of(i), :] = scores
        high = jnp.max(scores, axis=1, keepdims=True)
        rowx[0, me, i : i + 1, :] = to_lanes(high + jnp.log(jnp.sum(jnp.exp(scores - high), axis=1, keepdims=True)))
    row_pot = -log_sum_exp(row_exchange(0))

    high = None
    for i in range(nblocks):
        shifted = plan[rows_of(i), :] + to_rows(row_pot[i : i + 1, :])
        plan[rows_of(i), :] = shifted
        part = jnp.max(shifted, axis=0, keepdims=True)
        high = part if high is None else jnp.maximum(high, part)
    part = jnp.zeros_like(high)
    for i in range(nblocks):
        part = part + jnp.sum(jnp.exp(plan[rows_of(i), :] - high), axis=0, keepdims=True)
    col_send(0, high + jnp.log(part))
    col_pot = log_target - log_sum_exp(col_receive(0))

    for n in (1, 2):
        for i in range(nblocks):
            if n == 1:
                p = jnp.exp(plan[rows_of(i), :] + wide(col_pot))
            else:
                p = plan[rows_of(i), :] * wide(col_scale)
            plan[rows_of(i), :] = p
            rowx[n, me, i : i + 1, :] = to_lanes(jnp.sum(p, axis=1, keepdims=True))
        row_sum = add_up(row_exchange(n))
        row_pot = row_pot - jnp.log(row_sum)
        row_scale = 1.0 / row_sum
        part = None
        for i in range(nblocks):
            p = plan[rows_of(i), :] * to_rows(row_scale[i : i + 1, :])
            plan[rows_of(i), :] = p
            s = jnp.sum(p, axis=0, keepdims=True)
            part = s if part is None else part + s
        if n == 1:
            col_send(n, part)
            col_scale = target / add_up(col_receive(n))
            col_pot = col_pot + jnp.log(col_scale)

    col_send(2, part)
    sums = lax.dot_general(
        plan[...].astype(jnp.bfloat16), spans, (((0,), (0,)), ((), ())), preferred_element_type=jnp.float32
    )
    acc[...] = sums.reshape(acc.shape)

    def send_last(i, k, whole):
        last_out[i] = whole.astype(jnp.bfloat16)
        remote(last_out.at[i], last_in.at[i], ssem.at[LAST], rsem.at[LAST], z_peer(-STRIDE * k)).start()

    send_last(0, 4, acc[(a + 4) % NA, b])

    def send_window(*steps):
        for w, (k, d) in enumerate(WINDOW):
            if k in steps:
                stop = (z - d + NZ) % NZ
                win_out[w] = acc[(stop // STRIDE - k + NA) % NA, stop % STRIDE].astype(jnp.bfloat16)
                sem = WIN + ORDER.index(k)
                remote(win_out.at[w], win_in.at[w], ssem.at[sem], rsem.at[sem], z_peer(-d)).start()

    def gather_window(k):
        i = ORDER.index(k)
        lo = [w for w, (q, _) in enumerate(WINDOW) if q == k][0]
        drain(win_in.at[pl.ds(lo, len(SPREAD[k]))], rsem.at[WIN + i])
        whole = acc[(a - k + NA) % NA, b]
        for w in range(lo, lo + len(SPREAD[k])):
            whole = whole + win_in[w].astype(jnp.float32)
        if k != 0:
            send_last(i, k, whole)
        return whole

    send_window(3, -3)
    send_window(2, -2)
    gather_window(3)
    gather_window(-3)
    send_window(1, -1)
    gather_window(2)
    gather_window(-2)
    send_window(0)
    gather_window(1)
    gather_window(-1)
    whole = gather_window(0)

    rp_ref[...] = jnp.where(core == 0, row_pot[:4, :], row_pot[4:, :])
    col_sum = add_up(col_receive(2))
    pots[core] = col_pot + jnp.log(target / col_sum)
    remote(pots.at[core], pots.at[core], ssem.at[POT], rsem.at[POT], sibling).start()
    total[...] = col_sum
    line = total[pl.ds(z // 16, 1), :]
    wanted = lax.broadcasted_iota(jnp.int32, (8, BLOCK), 0) + (z % 16) * 8
    place = lax.broadcasted_iota(jnp.int32, (8, BLOCK), 1)
    mass = jnp.sum(jnp.where(place == wanted, line, 0.0), axis=1, keepdims=True)
    drain(pots.at[0], rsem.at[POT])
    for i in range(4):
        line = jnp.zeros((1, BLOCK), jnp.float32)
        for q in range(2):
            take = (down == (i % 2) * 64 + (lanes // 16) * 8 + lanes % 8) & (lanes // 8 % 2 == q)
            line = line + jnp.sum(jnp.where(take, to_rows(pots[q, i // 2 : i // 2 + 1, :]), 0.0), axis=0, keepdims=True)
        cp_ref[i : i + 1, :] = line

    drain(last_in, rsem.at[LAST])
    out = whole + jnp.sum(last_in[...].astype(jnp.float32), axis=0)
    newc_ref[...] = (out / mass).astype(jnp.bfloat16)

    drain(spans_all.at[0, pl.ds(0, NXY - 1)], ssem.at[SPANS])
    drain(spans_all.at[0], ssem.at[OTHER])
    drain(pat.at[0], ssem.at[PAT])
    drain(cent.at[:, pl.ds(0, 3)], ssem.at[CENT])
    for n in range(7):
        drain(chunk(0), ssem.at[STOP + n])
    for n in range(3):
        drain(rowx.at[n, pl.ds(0, 2 * NXY - 1)], ssem.at[ROW + n])
        drain(colx.at[n, pl.ds(0, NZ - 1)], ssem.at[COL + n])
    for i, k in enumerate(ORDER):
        if k != 4:
            drain(win_in.at[pl.ds(0, len(SPREAD[k]))], ssem.at[WIN + i])
    drain(pots.at[0], ssem.at[POT])
    drain(last_in, ssem.at[LAST])


def solution(mesh):
    def per_device(spans, centroids, pattern):
        width = spans.shape[1]
        f32, bf16 = jnp.float32, jnp.bfloat16
        target = (spans.shape[0] * mesh.size) / (centroids.shape[0] * mesh.size)
        args = [pltpu.with_memory_space_constraint(v, pltpu.HBM) for v in (spans, centroids, pattern)]
        vmem = pl.BlockSpec(memory_space=pltpu.VMEM)
        new, row_pot, col_pot = pl.pallas_call(
            functools.partial(kernel, math.log(target), target),
            name="sinkhorn",
            out_shape=(
                jax.ShapeDtypeStruct((8, width), bf16),
                jax.ShapeDtypeStruct((4, BLOCK), f32),
                jax.ShapeDtypeStruct((4, BLOCK), f32),
            ),
            in_specs=[pl.BlockSpec(memory_space=pltpu.HBM)] * 3,
            out_specs=(vmem,) * 3,
            scratch_shapes=[
                pltpu.VMEM((2, NXY, 32, width), bf16),
                pltpu.VMEM((NA, STRIDE, 8, width), bf16),
                pltpu.VMEM((2, 4, 16), jnp.int32),
                pltpu.VMEM((2 * NXY * 32, NZ * 8), f32),
                pltpu.VMEM((NA, STRIDE, 8, width), f32),
                pltpu.VMEM((len(WINDOW), 8, width), bf16),
                pltpu.VMEM((len(WINDOW), 8, width), bf16),
                pltpu.VMEM((NA - 1, 8, width), bf16),
                pltpu.VMEM((NA - 1, 8, width), bf16),
                pltpu.VMEM((3, 2 * NXY, 8, BLOCK), f32),
                pltpu.VMEM((3, NZ, 2, BLOCK), f32),
                pltpu.VMEM((2, 2, BLOCK), f32),
                pltpu.VMEM((2, BLOCK), f32),
                pltpu.SemaphoreType.DMA((NSEM,)),
                pltpu.SemaphoreType.DMA((NSEM,)),
                pltpu.SemaphoreType.DMA((3,)),
                pltpu.SemaphoreType.REGULAR,
            ],
            compiler_params=pltpu.CompilerParams(
                collective_id=0, has_side_effects=True, vmem_limit_bytes=32 * 1024 * 1024
            ),
        )(*args)
        return new, row_pot.reshape(-1), col_pot.reshape(-1)

    return jax.shard_map(
        per_device,
        mesh=mesh,
        in_specs=(P(("row", "col"), None), P(("col", "row"), None), P("row", None)),
        out_specs=(P(("col", "row"), None), P("row"), P("col")),
        check_vma=False,
    )
```

```python
import functools
import math

import jax
import jax.numpy as jnp
from jax import lax
from jax.experimental import pallas as pl
from jax.experimental.pallas import tpu as pltpu
from jax.sharding import PartitionSpec as P

MESH = pl.DeviceIdType.MESH
FLOOR = -1e30
SCALE = 0.0625
BLOCK = 128
NZ = 32
NXY = 16
STRIDE = 4
NA = NZ // STRIDE
SPREAD = {0: (2, -2, 1, -1), 1: (2, 1, -1), -1: (-2, 1, -1), 2: (2, 1, -1), -2: (-2, 1, -1), 3: (3, 2, 1, -1), -3: (-3, -2, 1, -1), 4: ()}
ORDER = (4, 3, -3, 2, -2, 1, -1, 0)
WINDOW = [(k, d) for k in ORDER for d in SPREAD[k]]
SPANS, OTHER, PAT, CENT, POT, LAST = range(6)
ROW, COL, STOP, WIN = 6, 9, 12, 19
COLW, COLF = 27, 28
NSEM = 29


def remote(src, dst, ssem, rsem, dev):
    return pltpu.make_async_remote_copy(
        src_ref=src, dst_ref=dst, send_sem=ssem, recv_sem=rsem, device_id=dev, device_id_type=MESH
    )


def drain(view, sem):
    pltpu.make_async_copy(view, view, sem).wait()


def kernel(
    log_target, target,
    sp_ref, ce_ref, pat_ref, out_ref,
    spans_all, cent, pat, plan, acc, win_out, win_in, last_out, last_in, rowx, colx, colw, colf, pots, total, ssem, rsem, lsem, hsem,
):
    width = sp_ref.shape[1]
    r, c = lax.axis_index("row"), lax.axis_index("col")
    z, core = r // 2, r % 2
    a, b = z // STRIDE, z % STRIDE
    x, y = c // 4, c % 4
    other = 1 - core
    sibling = (z * 2 + other, c)

    def z_peer(d):
        return (((z + d + NZ) % NZ) * 2 + core, c)

    def far_first(i):
        return (2 + ((i + 1) // 2) * (1 - 2 * (i % 2))) % 4

    def xy_peer(j, flip):
        return (z * 2 + (core + flip) % 2, ((x + far_first(j // 4)) % 4) * 4 + (y + far_first(j % 4)) % 4)

    def z_step(j):
        return 16 + ((j + 1) // 2) * (1 - 2 * (j % 2))

    def loop(n, fn):
        def step(i, carry):
            fn(i)
            return carry

        lax.fori_loop(0, n, step, 0)

    local = [
        pltpu.make_async_copy(ce_ref, cent.at[a, b], lsem.at[0]),
        pltpu.make_async_copy(sp_ref, spans_all.at[core, c], lsem.at[1]),
        pltpu.make_async_copy(pat_ref, pat.at[core], lsem.at[2]),
    ]
    for copy in local:
        copy.start()

    barrier = pltpu.get_barrier_semaphore()

    def greet(dev):
        pl.semaphore_signal(barrier, inc=1, device_id=dev, device_id_type=MESH)

    near = [d * s for d in (4, 3, 2, 1) for s in (1, -1)]
    for d in near:
        greet(z_peer(d))
    loop(NXY - 1, lambda j: greet(xy_peer(j, 0)))
    greet(sibling)
    pl.semaphore_wait(barrier, len(near) + NXY - 1 + 1)
    for d in (STRIDE, -STRIDE):
        pl.semaphore_signal(hsem, inc=1, device_id=z_peer(d), device_id_type=MESH)
    for copy in local:
        copy.wait()

    def chunk(k):
        return cent.at[(a - k + NA) % NA, b]

    def go(k, d, n):
        remote(chunk(k), chunk(k), ssem.at[STOP + n], rsem.at[STOP + n], z_peer(STRIDE * d)).start()

    def come(n):
        drain(chunk(0), rsem.at[STOP + n])

    def spread(k):
        for d in SPREAD[k]:
            remote(chunk(k), chunk(k), ssem.at[CENT], rsem.at[CENT], z_peer(d)).start()

    go(0, 1, 0)
    go(0, -1, 1)
    spread(0)
    mine = spans_all.at[core, c]
    loop(NXY - 1, lambda j: remote(mine, mine, ssem.at[SPANS], rsem.at[SPANS], xy_peer(j, 0)).start())
    remote(pat.at[core], pat.at[core], ssem.at[PAT], rsem.at[PAT], sibling).start()
    pl.semaphore_wait(hsem, 2)
    come(0)
    go(1, 2, 4)
    go(1, 1, 2)
    spread(1)
    come(1)
    go(-1, -2, 5)
    go(-1, -1, 3)
    spread(-1)
    come(2)
    spread(2)
    come(3)
    spread(-2)
    drain(spans_all.at[0, pl.ds(0, NXY - 1)], rsem.at[SPANS])
    remote(spans_all.at[core], spans_all.at[core], ssem.at[OTHER], rsem.at[OTHER], sibling).start()
    come(4)
    come(5)
    go(3 - 6 * core, 1 - 2 * core, 6)
    spread(3)
    spread(-3)
    come(6)
    drain(pat.at[0], rsem.at[PAT])
    drain(spans_all.at[0], rsem.at[OTHER])
    drain(cent.at[:, pl.ds(0, 3)], rsem.at[CENT])

    spans = spans_all[...].reshape(2 * NXY * 32, -1)
    table = cent[...].astype(jnp.float32).reshape(NZ * 8, -1).astype(jnp.bfloat16)
    nblocks = 8

    down = lax.broadcasted_iota(jnp.int32, (BLOCK, BLOCK), 0)
    lanes = lax.broadcasted_iota(jnp.int32, (BLOCK, BLOCK), 1)
    diagonal = down == lanes

    def to_lanes(v):
        return jnp.sum(jnp.where(diagonal, v, 0.0), axis=0, keepdims=True)

    def to_rows(v):
        return jnp.sum(jnp.where(diagonal, v, 0.0), axis=1, keepdims=True)

    def wide(v):
        return jnp.concatenate([v[0:1, :], v[1:2, :]], axis=1)

    def rows_of(k):
        return pl.ds(k * BLOCK, BLOCK)

    me = c * 2 + core

    def row_exchange(n):
        part = rowx.at[n, me]
        loop(
            2 * (NXY - 1),
            lambda j: remote(part, part, ssem.at[ROW + n], rsem.at[ROW + n], xy_peer(j // 2, j % 2)).start(),
        )
        remote(part, part, ssem.at[ROW + n], rsem.at[ROW + n], sibling).start()
        drain(rowx.at[n, pl.ds(0, 2 * NXY - 1)], rsem.at[ROW + n])
        return rowx[n]

    def col_send(n, part):
        colx[n, z, 0:1, :] = part[:, :BLOCK]
        colx[n, z, 1:2, :] = part[:, BLOCK:]
        piece = colx.at[n, z]
        loop(NZ - 1, lambda j: remote(piece, piece, ssem.at[COL + n], rsem.at[COL + n], z_peer(z_step(j))).start())

    def col_receive(n):
        drain(colx.at[n, pl.ds(0, NZ - 1)], rsem.at[COL + n])
        return colx[n]

    def log_sum_exp(v):
        high = jnp.max(v, axis=0)
        return high + jnp.log(jnp.sum(jnp.exp(v - high[None]), axis=0))

    def add_up(v):
        return jnp.sum(v, axis=0)

    block_of = lax.broadcasted_iota(jnp.int32, (1, NZ * 8), 1) // 64
    for i in range(nblocks):
        listed = pat[i // 4, i % 4 : i % 4 + 1, :]
        bias = jnp.zeros((1, NZ * 8), jnp.float32)
        for k in range(4):
            cell = jnp.max(jnp.where(listed == c * 4 + k, 0.0, FLOOR), axis=1, keepdims=True)
            bias = bias + jnp.where(block_of == k, cell, 0.0)
        scores = (
            lax.dot_general(
                spans[i * BLOCK : (i + 1) * BLOCK], table, (((1,), (1,)), ((), ())), preferred_element_type=jnp.float32
            )
            * SCALE
            + bias
        )
        plan[rows_of(i), :] = scores
        high = jnp.max(scores, axis=1, keepdims=True)
        rowx[0, me, i : i + 1, :] = to_lanes(high + jnp.log(jnp.sum(jnp.exp(scores - high), axis=1, keepdims=True)))
    row_pot = -log_sum_exp(row_exchange(0))

    high = None
    for i in range(nblocks):
        shifted = plan[rows_of(i), :] + to_rows(row_pot[i : i + 1, :])
        plan[rows_of(i), :] = shifted
        part = jnp.max(shifted, axis=0, keepdims=True)
        high = part if high is None else jnp.maximum(high, part)
    part = jnp.zeros_like(high)
    for i in range(nblocks):
        part = part + jnp.sum(jnp.exp(plan[rows_of(i), :] - high), axis=0, keepdims=True)
    col_send(0, high + jnp.log(part))
    col_pot = log_target - log_sum_exp(col_receive(0))

    for n in (1, 2):
        for i in range(nblocks):
            if n == 1:
                p = jnp.exp(plan[rows_of(i), :] + wide(col_pot))
            else:
                p = plan[rows_of(i), :] * wide(col_scale)
            plan[rows_of(i), :] = p
            rowx[n, me, i : i + 1, :] = to_lanes(jnp.sum(p, axis=1, keepdims=True))
        row_sum = add_up(row_exchange(n))
        row_pot = row_pot - jnp.log(row_sum)
        row_scale = 1.0 / row_sum
        part = None
        for i in range(nblocks):
            p = plan[rows_of(i), :] * to_rows(row_scale[i : i + 1, :])
            plan[rows_of(i), :] = p
            s = jnp.sum(p, axis=0, keepdims=True)
            part = s if part is None else part + s
        if n == 1:
            col_send(n, part)
            col_scale = target / add_up(col_receive(n))
            col_pot = col_pot + jnp.log(col_scale)

    colw[3, 0:1, :] = part[:, :BLOCK]
    colw[3, 1:2, :] = part[:, BLOCK:]
    for i, d in enumerate((2, 1, -1)):
        remote(colw.at[3], colw.at[i], ssem.at[COLW], rsem.at[COLW], z_peer(d)).start()

    sums = lax.dot_general(
        plan[...].astype(jnp.bfloat16), spans, (((0,), (0,)), ((), ())), preferred_element_type=jnp.float32
    )
    acc[...] = sums.reshape(acc.shape)

    def send_last(i, k, whole):
        last_out[i] = whole.astype(jnp.bfloat16)
        remote(last_out.at[i], last_in.at[i], ssem.at[LAST], rsem.at[LAST], z_peer(-STRIDE * k)).start()

    send_last(0, 4, acc[(a + 4) % NA, b])

    def send_window(*steps):
        for w, (k, d) in enumerate(WINDOW):
            if k in steps:
                stop = (z - d + NZ) % NZ
                win_out[w] = acc[(stop // STRIDE - k + NA) % NA, stop % STRIDE].astype(jnp.bfloat16)
                sem = WIN + ORDER.index(k)
                remote(win_out.at[w], win_in.at[w], ssem.at[sem], rsem.at[sem], z_peer(-d)).start()

    def gather_window(k):
        i = ORDER.index(k)
        lo = [w for w, (q, _) in enumerate(WINDOW) if q == k][0]
        drain(win_in.at[pl.ds(lo, len(SPREAD[k]))], rsem.at[WIN + i])
        whole = acc[(a - k + NA) % NA, b]
        for w in range(lo, lo + len(SPREAD[k])):
            whole = whole + win_in[w].astype(jnp.float32)
        if k != 0:
            send_last(i, k, whole)
        return whole

    send_window(3, -3)
    send_window(2, -2)
    drain(colw.at[pl.ds(0, 3)], rsem.at[COLW])
    colf[NA - 1] = add_up(colw[...])
    for i, k in enumerate((4, 3, -3, 2, -2, 1, -1)):
        remote(colf.at[NA - 1], colf.at[i], ssem.at[COLF], rsem.at[COLF], z_peer(-STRIDE * k)).start()
    gather_window(3)
    gather_window(-3)
    send_window(1, -1)
    gather_window(2)
    gather_window(-2)
    send_window(0)
    gather_window(1)
    gather_window(-1)
    whole = gather_window(0)

    out_ref[0:4, width:] = jnp.where(core == 0, row_pot[:4, :], row_pot[4:, :])
    drain(colf.at[pl.ds(0, NA - 1)], rsem.at[COLF])
    col_sum = add_up(colf[...])
    pots[core] = col_pot + jnp.log(target / col_sum)
    remote(pots.at[core], pots.at[core], ssem.at[POT], rsem.at[POT], sibling).start()
    total[...] = col_sum
    line = total[pl.ds(z // 16, 1), :]
    wanted = lax.broadcasted_iota(jnp.int32, (8, BLOCK), 0) + (z % 16) * 8
    place = lax.broadcasted_iota(jnp.int32, (8, BLOCK), 1)
    mass = jnp.sum(jnp.where(place == wanted, line, 0.0), axis=1, keepdims=True)
    drain(pots.at[0], rsem.at[POT])
    for i in range(4):
        line = jnp.zeros((1, BLOCK), jnp.float32)
        for q in range(2):
            take = (down == (i % 2) * 64 + (lanes // 16) * 8 + lanes % 8) & (lanes // 8 % 2 == q)
            line = line + jnp.sum(jnp.where(take, to_rows(pots[q, i // 2 : i // 2 + 1, :]), 0.0), axis=0, keepdims=True)
        out_ref[4 + i : 5 + i, width:] = line

    drain(last_in, rsem.at[LAST])
    out = whole + jnp.sum(last_in[...].astype(jnp.float32), axis=0)
    out_ref[:, :width] = out / mass

    drain(spans_all.at[0, pl.ds(0, NXY - 1)], ssem.at[SPANS])
    drain(spans_all.at[0], ssem.at[OTHER])
    drain(pat.at[0], ssem.at[PAT])
    drain(cent.at[:, pl.ds(0, 3)], ssem.at[CENT])
    for n in range(7):
        drain(chunk(0), ssem.at[STOP + n])
    for n in range(3):
        drain(rowx.at[n, pl.ds(0, 2 * NXY - 1)], ssem.at[ROW + n])
    for n in range(2):
        drain(colx.at[n, pl.ds(0, NZ - 1)], ssem.at[COL + n])
    drain(colw.at[pl.ds(0, 3)], ssem.at[COLW])
    drain(colf.at[pl.ds(0, NA - 1)], ssem.at[COLF])
    for i, k in enumerate(ORDER):
        if k != 4:
            drain(win_in.at[pl.ds(0, len(SPREAD[k]))], ssem.at[WIN + i])
    drain(pots.at[0], ssem.at[POT])
    drain(last_in, ssem.at[LAST])


def solution(mesh):
    def per_device(spans, centroids, pattern):
        width = spans.shape[1]
        f32, bf16 = jnp.float32, jnp.bfloat16
        target = (spans.shape[0] * mesh.size) / (centroids.shape[0] * mesh.size)
        args = [pltpu.with_memory_space_constraint(v, pltpu.HBM) for v in (spans, centroids, pattern)]
        packed = pl.pallas_call(
            functools.partial(kernel, math.log(target), target),
            name="sinkhorn",
            out_shape=jax.ShapeDtypeStruct((8, width + BLOCK), f32),
            in_specs=[pl.BlockSpec(memory_space=pltpu.HBM)] * 3,
            out_specs=pl.BlockSpec(memory_space=pltpu.VMEM),
            scratch_shapes=[
                pltpu.VMEM((2, NXY, 32, width), bf16),
                pltpu.VMEM((NA, STRIDE, 8, width), bf16),
                pltpu.VMEM((2, 4, 16), jnp.int32),
                pltpu.VMEM((2 * NXY * 32, NZ * 8), f32),
                pltpu.VMEM((NA, STRIDE, 8, width), f32),
                pltpu.VMEM((len(WINDOW), 8, width), bf16),
                pltpu.VMEM((len(WINDOW), 8, width), bf16),
                pltpu.VMEM((NA - 1, 8, width), bf16),
                pltpu.VMEM((NA - 1, 8, width), bf16),
                pltpu.VMEM((3, 2 * NXY, 8, BLOCK), f32),
                pltpu.VMEM((2, NZ, 2, BLOCK), f32),
                pltpu.VMEM((4, 2, BLOCK), f32),
                pltpu.VMEM((NA, 2, BLOCK), f32),
                pltpu.VMEM((2, 2, BLOCK), f32),
                pltpu.VMEM((2, BLOCK), f32),
                pltpu.SemaphoreType.DMA((NSEM,)),
                pltpu.SemaphoreType.DMA((NSEM,)),
                pltpu.SemaphoreType.DMA((3,)),
                pltpu.SemaphoreType.REGULAR,
            ],
            compiler_params=pltpu.CompilerParams(
                collective_id=0, has_side_effects=True, vmem_limit_bytes=32 * 1024 * 1024
            ),
        )(*args)
        pots = packed[:, width:]
        return packed[:, :width].astype(bf16), pots[:4].reshape(-1), pots[4:].reshape(-1)

    return jax.shard_map(
        per_device,
        mesh=mesh,
        in_specs=(P(("row", "col"), None), P(("col", "row"), None), P("row", None)),
        out_specs=(P(("col", "row"), None), P("row"), P("col")),
        check_vma=False,
    )
```

```python
import functools
import math

import jax
import jax.numpy as jnp
from jax import lax
from jax.experimental import pallas as pl
from jax.experimental.pallas import tpu as pltpu
from jax.sharding import PartitionSpec as P

MESH = pl.DeviceIdType.MESH
FLOOR = -1e30
SCALE = 0.0625
BLOCK = 128
NZ = 32
NXY = 16
STRIDE = 4
NA = NZ // STRIDE
SPREAD = {0: (2, -2, 1, -1), 1: (2, 1, -1), -1: (-2, 1, -1), 2: (2, 1, -1), -2: (-2, 1, -1), 3: (3, 2, 1, -1), -3: (-3, -2, 1, -1), 4: ()}
ORDER = (4, 3, -3, 2, -2, 1, -1, 0)
WINDOW = [(k, d) for k in ORDER for d in SPREAD[k]]
SPANS, OTHER, PAT, CENT, POT, LAST = range(6)
ROW, COL, STOP, WIN = 6, 9, 12, 19
COLW, COLF, FAR = 27, 28, 29
NSEM = 30


def remote(src, dst, ssem, rsem, dev):
    return pltpu.make_async_remote_copy(
        src_ref=src, dst_ref=dst, send_sem=ssem, recv_sem=rsem, device_id=dev, device_id_type=MESH
    )


def drain(view, sem):
    pltpu.make_async_copy(view, view, sem).wait()


def kernel(
    log_target, target,
    sp_ref, ce_ref, pat_ref, out_ref,
    spans_all, cent, pat, plan, acc, win_out, win_in, last_out, last_in, rowx, colx, colw, colf, pots, total, ssem, rsem, lsem, hsem,
):
    width = sp_ref.shape[1]
    r, c = lax.axis_index("row"), lax.axis_index("col")
    z, core = r // 2, r % 2
    a, b = z // STRIDE, z % STRIDE
    x, y = c // 4, c % 4
    other = 1 - core
    sibling = (z * 2 + other, c)

    def z_peer(d):
        return (((z + d + NZ) % NZ) * 2 + core, c)

    def far_first(i):
        return (2 + ((i + 1) // 2) * (1 - 2 * (i % 2))) % 4

    def xy_peer(j, flip):
        return (z * 2 + (core + flip) % 2, ((x + far_first(j // 4)) % 4) * 4 + (y + far_first(j % 4)) % 4)

    def z_step(j):
        return 16 + ((j + 1) // 2) * (1 - 2 * (j % 2))

    def loop(n, fn):
        def step(i, carry):
            fn(i)
            return carry

        lax.fori_loop(0, n, step, 0)

    local = [
        pltpu.make_async_copy(ce_ref, cent.at[a, b], lsem.at[0]),
        pltpu.make_async_copy(sp_ref, spans_all.at[core, c], lsem.at[1]),
        pltpu.make_async_copy(pat_ref, pat.at[core], lsem.at[2]),
    ]
    for copy in local:
        copy.start()

    barrier = pltpu.get_barrier_semaphore()

    def greet(dev):
        pl.semaphore_signal(barrier, inc=1, device_id=dev, device_id_type=MESH)

    near = [d * s for d in (4, 3, 2, 1) for s in (1, -1)]
    for d in near:
        greet(z_peer(d))
    loop(NXY - 1, lambda j: greet(xy_peer(j, 0)))
    greet(sibling)
    pl.semaphore_wait(barrier, len(near) + NXY - 1 + 1)
    for d in (STRIDE, -STRIDE):
        pl.semaphore_signal(hsem, inc=1, device_id=z_peer(d), device_id_type=MESH)
    for copy in local:
        copy.wait()

    def chunk(k):
        return cent.at[(a - k + NA) % NA, b]

    def go(k, d, n):
        remote(chunk(k), chunk(k), ssem.at[STOP + n], rsem.at[STOP + n], z_peer(STRIDE * d)).start()

    def come(n):
        drain(chunk(0), rsem.at[STOP + n])

    def spread(k):
        for d in SPREAD[k]:
            remote(chunk(k), chunk(k), ssem.at[CENT], rsem.at[CENT], z_peer(d)).start()

    go(0, 1, 0)
    go(0, -1, 1)
    spread(0)
    mine = spans_all.at[core, c]
    loop(NXY - 1, lambda j: remote(mine, mine, ssem.at[SPANS], rsem.at[SPANS], xy_peer(j, 0)).start())
    remote(pat.at[core], pat.at[core], ssem.at[PAT], rsem.at[PAT], sibling).start()
    pl.semaphore_wait(hsem, 2)
    come(0)
    go(1, 2, 4)
    go(1, 1, 2)
    spread(1)
    come(1)
    go(-1, -2, 5)
    go(-1, -1, 3)
    spread(-1)
    come(2)
    spread(2)
    come(3)
    spread(-2)
    drain(spans_all.at[0, pl.ds(0, NXY - 1)], rsem.at[SPANS])
    remote(spans_all.at[core], spans_all.at[core], ssem.at[OTHER], rsem.at[OTHER], sibling).start()
    come(4)
    come(5)
    go(3 - 6 * core, 1 - 2 * core, 6)
    spread(3)
    spread(-3)
    come(6)
    drain(pat.at[0], rsem.at[PAT])
    drain(spans_all.at[0], rsem.at[OTHER])
    drain(cent.at[:, pl.ds(0, 3)], rsem.at[CENT])

    spans = spans_all[...].reshape(2 * NXY * 32, -1)
    table = cent[...].astype(jnp.float32).reshape(NZ * 8, -1).astype(jnp.bfloat16)
    nblocks = 8

    down = lax.broadcasted_iota(jnp.int32, (BLOCK, BLOCK), 0)
    lanes = lax.broadcasted_iota(jnp.int32, (BLOCK, BLOCK), 1)
    diagonal = down == lanes

    def to_lanes(v):
        return jnp.sum(jnp.where(diagonal, v, 0.0), axis=0, keepdims=True)

    def to_rows(v):
        return jnp.sum(jnp.where(diagonal, v, 0.0), axis=1, keepdims=True)

    def wide(v):
        return jnp.concatenate([v[0:1, :], v[1:2, :]], axis=1)

    def rows_of(k):
        return pl.ds(k * BLOCK, BLOCK)

    me = c * 2 + core

    def row_exchange(n):
        part = rowx.at[n, me]
        loop(
            2 * (NXY - 1),
            lambda j: remote(part, part, ssem.at[ROW + n], rsem.at[ROW + n], xy_peer(j // 2, j % 2)).start(),
        )
        remote(part, part, ssem.at[ROW + n], rsem.at[ROW + n], sibling).start()
        drain(rowx.at[n, pl.ds(0, 2 * NXY - 1)], rsem.at[ROW + n])
        return rowx[n]

    def col_send(n, part):
        colx[n, z, 0:1, :] = part[:, :BLOCK]
        colx[n, z, 1:2, :] = part[:, BLOCK:]
        piece = colx.at[n, z]
        loop(NZ - 1, lambda j: remote(piece, piece, ssem.at[COL + n], rsem.at[COL + n], z_peer(z_step(j))).start())

    def col_receive(n):
        drain(colx.at[n, pl.ds(0, NZ - 1)], rsem.at[COL + n])
        return colx[n]

    def log_sum_exp(v):
        high = jnp.max(v, axis=0)
        return high + jnp.log(jnp.sum(jnp.exp(v - high[None]), axis=0))

    def add_up(v):
        return jnp.sum(v, axis=0)

    block_of = lax.broadcasted_iota(jnp.int32, (1, NZ * 8), 1) // 64
    for i in range(nblocks):
        listed = pat[i // 4, i % 4 : i % 4 + 1, :]
        bias = jnp.zeros((1, NZ * 8), jnp.float32)
        for k in range(4):
            cell = jnp.max(jnp.where(listed == c * 4 + k, 0.0, FLOOR), axis=1, keepdims=True)
            bias = bias + jnp.where(block_of == k, cell, 0.0)
        scores = (
            lax.dot_general(
                spans[i * BLOCK : (i + 1) * BLOCK], table, (((1,), (1,)), ((), ())), preferred_element_type=jnp.float32
            )
            * SCALE
            + bias
        )
        plan[rows_of(i), :] = scores
        high = jnp.max(scores, axis=1, keepdims=True)
        rowx[0, me, i : i + 1, :] = to_lanes(high + jnp.log(jnp.sum(jnp.exp(scores - high), axis=1, keepdims=True)))
    row_pot = -log_sum_exp(row_exchange(0))

    high = None
    for i in range(nblocks):
        shifted = plan[rows_of(i), :] + to_rows(row_pot[i : i + 1, :])
        plan[rows_of(i), :] = shifted
        part = jnp.max(shifted, axis=0, keepdims=True)
        high = part if high is None else jnp.maximum(high, part)
    part = jnp.zeros_like(high)
    for i in range(nblocks):
        part = part + jnp.sum(jnp.exp(plan[rows_of(i), :] - high), axis=0, keepdims=True)
    col_send(0, high + jnp.log(part))
    col_pot = log_target - log_sum_exp(col_receive(0))

    for n in (1, 2):
        for i in range(nblocks):
            if n == 1:
                p = jnp.exp(plan[rows_of(i), :] + wide(col_pot))
            else:
                p = plan[rows_of(i), :] * wide(col_scale)
            plan[rows_of(i), :] = p
            rowx[n, me, i : i + 1, :] = to_lanes(jnp.sum(p, axis=1, keepdims=True))
        row_sum = add_up(row_exchange(n))
        row_pot = row_pot - jnp.log(row_sum)
        row_scale = 1.0 / row_sum
        part = None
        for i in range(nblocks):
            p = plan[rows_of(i), :] * to_rows(row_scale[i : i + 1, :])
            plan[rows_of(i), :] = p
            s = jnp.sum(p, axis=0, keepdims=True)
            part = s if part is None else part + s
        if n == 1:
            col_send(n, part)
            col_scale = target / add_up(col_receive(n))
            col_pot = col_pot + jnp.log(col_scale)

    colw[3, 0:1, :] = part[:, :BLOCK]
    colw[3, 1:2, :] = part[:, BLOCK:]
    for i, d in enumerate((2, 1, -1)):
        remote(colw.at[3], colw.at[i], ssem.at[COLW], rsem.at[COLW], z_peer(d)).start()

    sums = lax.dot_general(
        plan[...].astype(jnp.bfloat16), spans, (((0,), (0,)), ((), ())), preferred_element_type=jnp.float32
    )
    acc[...] = sums.reshape(acc.shape)

    def send_last(i, k, whole):
        last_out[i] = whole.astype(jnp.bfloat16)
        remote(last_out.at[i], last_in.at[i], ssem.at[LAST], rsem.at[LAST], z_peer(-STRIDE * k)).start()

    last_out[0] = acc[(a + 4) % NA, b].astype(jnp.bfloat16)
    remote(last_out.at[0], last_in.at[0], ssem.at[FAR], rsem.at[FAR], z_peer(STRIDE * (4 * core - 2))).start()

    def send_window(*steps):
        for w, (k, d) in enumerate(WINDOW):
            if k in steps:
                stop = (z - d + NZ) % NZ
                win_out[w] = acc[(stop // STRIDE - k + NA) % NA, stop % STRIDE].astype(jnp.bfloat16)
                sem = WIN + ORDER.index(k)
                remote(win_out.at[w], win_in.at[w], ssem.at[sem], rsem.at[sem], z_peer(-d)).start()

    def gather_window(k):
        i = ORDER.index(k)
        lo = [w for w, (q, _) in enumerate(WINDOW) if q == k][0]
        drain(win_in.at[pl.ds(lo, len(SPREAD[k]))], rsem.at[WIN + i])
        whole = acc[(a - k + NA) % NA, b]
        for w in range(lo, lo + len(SPREAD[k])):
            whole = whole + win_in[w].astype(jnp.float32)
        if abs(k) == 2:
            whole = whole + jnp.where(core == (2 - k) // 4, last_in[0].astype(jnp.float32), 0.0)
        if k != 0:
            send_last(i, k, whole)
        return whole

    send_window(3, -3)
    send_window(2, -2)
    drain(colw.at[pl.ds(0, 3)], rsem.at[COLW])
    colf[NA - 1] = add_up(colw[...])
    for i, k in enumerate((4, 3, -3, 2, -2, 1, -1)):
        remote(colf.at[NA - 1], colf.at[i], ssem.at[COLF], rsem.at[COLF], z_peer(-STRIDE * k)).start()
    gather_window(3)
    gather_window(-3)
    send_window(1, -1)
    drain(last_in.at[0], rsem.at[FAR])
    gather_window(2)
    gather_window(-2)
    send_window(0)
    gather_window(1)
    gather_window(-1)
    whole = gather_window(0)

    out_ref[0:4, width:] = jnp.where(core == 0, row_pot[:4, :], row_pot[4:, :])
    drain(colf.at[pl.ds(0, NA - 1)], rsem.at[COLF])
    col_sum = add_up(colf[...])
    pots[core] = col_pot + jnp.log(target / col_sum)
    remote(pots.at[core], pots.at[core], ssem.at[POT], rsem.at[POT], sibling).start()
    total[...] = col_sum
    line = total[pl.ds(z // 16, 1), :]
    wanted = lax.broadcasted_iota(jnp.int32, (8, BLOCK), 0) + (z % 16) * 8
    place = lax.broadcasted_iota(jnp.int32, (8, BLOCK), 1)
    mass = jnp.sum(jnp.where(place == wanted, line, 0.0), axis=1, keepdims=True)
    drain(pots.at[0], rsem.at[POT])
    for i in range(4):
        line = jnp.zeros((1, BLOCK), jnp.float32)
        for q in range(2):
            take = (down == (i % 2) * 64 + (lanes // 16) * 8 + lanes % 8) & (lanes // 8 % 2 == q)
            line = line + jnp.sum(jnp.where(take, to_rows(pots[q, i // 2 : i // 2 + 1, :]), 0.0), axis=0, keepdims=True)
        out_ref[4 + i : 5 + i, width:] = line

    drain(last_in.at[pl.ds(1, NA - 2)], rsem.at[LAST])
    out = whole + jnp.sum(last_in[1 : NA - 1].astype(jnp.float32), axis=0)
    out_ref[:, :width] = out / mass

    drain(spans_all.at[0, pl.ds(0, NXY - 1)], ssem.at[SPANS])
    drain(spans_all.at[0], ssem.at[OTHER])
    drain(pat.at[0], ssem.at[PAT])
    drain(cent.at[:, pl.ds(0, 3)], ssem.at[CENT])
    for n in range(7):
        drain(chunk(0), ssem.at[STOP + n])
    for n in range(3):
        drain(rowx.at[n, pl.ds(0, 2 * NXY - 1)], ssem.at[ROW + n])
    for n in range(2):
        drain(colx.at[n, pl.ds(0, NZ - 1)], ssem.at[COL + n])
    drain(colw.at[pl.ds(0, 3)], ssem.at[COLW])
    drain(colf.at[pl.ds(0, NA - 1)], ssem.at[COLF])
    for i, k in enumerate(ORDER):
        if k != 4:
            drain(win_in.at[pl.ds(0, len(SPREAD[k]))], ssem.at[WIN + i])
    drain(pots.at[0], ssem.at[POT])
    drain(last_in.at[pl.ds(1, NA - 2)], ssem.at[LAST])
    drain(last_in.at[0], ssem.at[FAR])


def solution(mesh):
    def per_device(spans, centroids, pattern):
        width = spans.shape[1]
        f32, bf16 = jnp.float32, jnp.bfloat16
        target = (spans.shape[0] * mesh.size) / (centroids.shape[0] * mesh.size)
        args = [pltpu.with_memory_space_constraint(v, pltpu.HBM) for v in (spans, centroids, pattern)]
        packed = pl.pallas_call(
            functools.partial(kernel, math.log(target), target),
            name="sinkhorn",
            out_shape=jax.ShapeDtypeStruct((8, width + BLOCK), f32),
            in_specs=[pl.BlockSpec(memory_space=pltpu.HBM)] * 3,
            out_specs=pl.BlockSpec(memory_space=pltpu.VMEM),
            scratch_shapes=[
                pltpu.VMEM((2, NXY, 32, width), bf16),
                pltpu.VMEM((NA, STRIDE, 8, width), bf16),
                pltpu.VMEM((2, 4, 16), jnp.int32),
                pltpu.VMEM((2 * NXY * 32, NZ * 8), f32),
                pltpu.VMEM((NA, STRIDE, 8, width), f32),
                pltpu.VMEM((len(WINDOW), 8, width), bf16),
                pltpu.VMEM((len(WINDOW), 8, width), bf16),
                pltpu.VMEM((NA - 1, 8, width), bf16),
                pltpu.VMEM((NA - 1, 8, width), bf16),
                pltpu.VMEM((3, 2 * NXY, 8, BLOCK), f32),
                pltpu.VMEM((2, NZ, 2, BLOCK), f32),
                pltpu.VMEM((4, 2, BLOCK), f32),
                pltpu.VMEM((NA, 2, BLOCK), f32),
                pltpu.VMEM((2, 2, BLOCK), f32),
                pltpu.VMEM((2, BLOCK), f32),
                pltpu.SemaphoreType.DMA((NSEM,)),
                pltpu.SemaphoreType.DMA((NSEM,)),
                pltpu.SemaphoreType.DMA((3,)),
                pltpu.SemaphoreType.REGULAR,
            ],
            compiler_params=pltpu.CompilerParams(
                collective_id=0, has_side_effects=True, vmem_limit_bytes=32 * 1024 * 1024
            ),
        )(*args)
        pots = packed[:, width:]
        return packed[:, :width].astype(bf16), pots[:4].reshape(-1), pots[4:].reshape(-1)

    return jax.shard_map(
        per_device,
        mesh=mesh,
        in_specs=(P(("row", "col"), None), P(("col", "row"), None), P("row", None)),
        out_specs=(P(("col", "row"), None), P("row"), P("col")),
        check_vma=False,
    )
```
